256 devices in a mesh: drift: 16 (over x_lo, y, core), wire: 16 (over x_hi, z).
Axes of the slice: x: 4 (x_hi: 2, x_lo: 2; x = x_hi * 2 + x_lo), y: 4, z: 8, core: 2. Of those that a mesh axis runs over, the one named last changes fastest.
Arguments:
- features: bfloat16 [16, 16, 576, 128], P('drift', 'wire'), may hold values from -6 to 6
- first_weight: bfloat16 [27, 128, 128], replicated, may hold values from -0.109375 to 0.109375
- second_weight: bfloat16 [27, 128, 128], replicated, may hold values from -0.109375 to 0.109375
- cotangent: bfloat16 [16, 16, 576, 128], P('drift', 'wire'), may hold values from -6 to 6
- counts: int32 [16, 16], P('drift', 'wire'), may hold values from 1 to 9, as said below
- kernel_map: int32 [16, 16, 27, 9], P('drift', 'wire'), may hold values from 0 to 25, as said below
- send_lists: int32 [16, 16, 16], P('drift', 'wire'), may hold values from 0 to 9, as said below
Outputs:
- output: bfloat16 [16, 16, 576, 128], P('drift', 'wire')
- grad_features: bfloat16 [16, 16, 576, 128], P('drift', 'wire')
- grad_first: float32 [27, 128, 128], replicated
- grad_second: float32 [27, 128, 128], replicated
The draws below stay inside these ranges and needn't reach their ends.
Inputs may be any that keep to these rules, and one draw needn't show every extreme that they name: Slots below counts[i, j] hold the region's active blocks in order of position; some region has all 9 positions active and some region exactly one. kernel_map[i, j, k, s] is the block_table row of the active block at block offset k of slot s: a slot below 9 for a block of the same region, 10 + a segment position for a block of a neighbouring region (listed there in that region's send list), and 9 where that block is inactive, outside the volume, or s is an empty slot. `send_lists`: each segment lists, in order of position, the positions of the region's face, edge or corner next to that neighbour: the slot of an active block there, else 9.
All inputs are finite; a program needn't handle non-finite values.
Results may differ from the reference program's by a relative error of at most 0.0031.
Values may be sent and summed in bfloat16 or wider, within the bound.
A program may use at most 128 MiB of HBM per device.

```python
import math
import jax
import jax.numpy as jnp
import numpy as np
from jax import lax

C = 128
BX = 3
BW = 3
BZ = 1
DRIFT_PARTS = 16
WIRE_PARTS = 16
NB = 9
VOXELS = 147456


DIRECTIONS = ((-1, 0), (1, 0), (0, -1), (0, 1), (-1, -1), (-1, 1), (1, -1), (1, 1))


def segment_length_drawn(drift_step, wire_step):
    return (BX if drift_step == 0 else 1) * (BW if wire_step == 0 else 1) * BZ


def segment_start_drawn(drift_step, wire_step):
    first_row = 0
    for direction in DIRECTIONS:
        if direction == (drift_step, wire_step):
            return first_row
        first_row = first_row + segment_length_drawn(direction[0], direction[1])
    return first_row


def face_positions(drift_step, wire_step):
    if drift_step == 1:
        drift_cells = [BX - 1]
    elif drift_step == -1:
        drift_cells = [0]
    else:
        drift_cells = list(range(BX))
    if wire_step == 1:
        wire_cells = [BW - 1]
    elif wire_step == -1:
        wire_cells = [0]
    else:
        wire_cells = list(range(BW))
    listed = []
    for drift_cell in drift_cells:
        for wire_cell in wire_cells:
            for depth_cell in range(BZ):
                listed.append((drift_cell * BW + wire_cell) * BZ + depth_cell)
    return listed


def offset_tables():
    region_size = BX * BW * BZ
    near_pos = np.zeros((27, region_size), np.int32)
    shift_ids = np.zeros((27, region_size), np.int32)
    halo_ids = np.zeros((27, region_size), np.int32)
    is_local = np.zeros((27, region_size), bool)
    depth_ok = np.zeros((27, region_size), bool)
    for offset in range(27):
        step_x = offset // 9 - 1
        step_y = offset // 3 % 3 - 1
        step_z = offset % 3 - 1
        for position in range(region_size):
            drift_cell = position // (BW * BZ)
            wire_cell = position // BZ % BW
            depth_cell = position % BZ
            target_drift = drift_cell + step_x
            drift_move = -1 if target_drift < 0 else 1 if target_drift >= BX else 0
            target_drift = target_drift - drift_move * BX
            target_wire = wire_cell + step_y
            wire_move = -1 if target_wire < 0 else 1 if target_wire >= BW else 0
            target_wire = target_wire - wire_move * BW
            target_depth = depth_cell + step_z
            inside_depth = 0 <= target_depth < BZ
            depth_value = target_depth if inside_depth else 0
            near_pos[offset, position] = (target_drift * BW + target_wire) * BZ + depth_value
            shift_ids[offset, position] = (drift_move + 1) * 3 + (wire_move + 1)
            is_local[offset, position] = drift_move == 0 and wire_move == 0
            depth_ok[offset, position] = inside_depth
            if drift_move != 0 or wire_move != 0:
                column_index = target_drift if drift_move == 0 else 0
                wire_count = BW if wire_move == 0 else 1
                row_index = target_wire if wire_move == 0 else 0
                halo_ids[offset, position] = segment_start_drawn(drift_move, wire_move) + (column_index * wire_count + row_index) * BZ + depth_value
    return (near_pos, shift_ids, halo_ids, is_local, depth_ok)


def geometry(key):
    base = jax.random.fold_in(key, 31)
    key_level, key_drift, key_wire, key_roll, key_seed = jax.random.split(base, 5)
    drift_parts = DRIFT_PARTS
    wire_parts = WIRE_PARTS
    region_size = BX * BW * BZ
    levels = jax.random.randint(key_level, (drift_parts, wire_parts), 2, 10)
    full_drift = jax.random.randint(key_drift, (), 1, drift_parts)
    full_wire = jax.random.randint(key_wire, (), 1, wire_parts)
    drift_ids = jnp.arange(drift_parts, dtype=jnp.int32)[:, None]
    wire_ids = jnp.arange(wire_parts, dtype=jnp.int32)[None, :]
    is_full = (drift_ids == full_drift) & (wire_ids == full_wire)
    is_single = (drift_ids == 0) & (wire_ids == wire_parts - 1)
    is_corner = (drift_ids == full_drift - 1) & (wire_ids == full_wire - 1)
    is_anchor = (drift_ids == 0) & (wire_ids == 0)
    levels = jnp.where(is_full, 16, jnp.where(is_single, 0, levels))
    rolls = jax.random.randint(key_roll, (drift_parts, wire_parts, region_size), 0, 16)
    seeds = jax.random.randint(key_seed, (drift_parts, wire_parts), 0, region_size)
    seeds = jnp.where(is_corner | is_anchor, region_size - 1, seeds)
    positions = jnp.arange(region_size, dtype=jnp.int32)
    off_position = (BX - 1) * BW * BZ
    active = (rolls < levels[:, :, None]) | (positions[None, None, :] == seeds[:, :, None])
    active = active & jnp.logical_not(is_anchor[:, :, None] & (positions[None, None, :] == off_position))
    active_ints = active.astype(jnp.int32)
    counts = jnp.sum(active_ints, axis=2).astype(jnp.int32)
    slot_of_pos = jnp.where(active, jnp.cumsum(active_ints, axis=2) - 1, NB).astype(jnp.int32)
    near_pos, shift_ids, halo_ids, is_local, depth_ok = offset_tables()
    padded = jnp.pad(active, ((1, 1), (1, 1), (0, 0)))
    stacks = []
    for drift_move in (-1, 0, 1):
        for wire_move in (-1, 0, 1):
            stacks.append(padded[1 + drift_move:1 + drift_move + drift_parts, 1 + wire_move:1 + wire_move + wire_parts])
    near_active = jnp.stack(stacks, axis=2)
    local_slot = slot_of_pos[:, :, jnp.asarray(near_pos)]
    remote_ok = near_active[:, :, jnp.asarray(shift_ids), jnp.asarray(near_pos)]
    map_pos = jnp.where(jnp.asarray(is_local), local_slot, jnp.where(remote_ok, NB + 1 + jnp.asarray(halo_ids), NB))
    map_pos = jnp.where(jnp.asarray(depth_ok), map_pos, NB).astype(jnp.int32)
    slot_ids = jnp.arange(NB, dtype=jnp.int32)
    matches = slot_of_pos[:, :, None, :] == slot_ids[None, None, :, None]
    pos_of_slot = jnp.sum(jnp.where(matches, positions[None, None, None, :], 0), axis=3).astype(jnp.int32)
    index_rows = jnp.broadcast_to(pos_of_slot[:, :, None, :], (drift_parts, wire_parts, 27, NB))
    gathered = jnp.take_along_axis(map_pos, index_rows, axis=3)
    live_slots = slot_ids[None, None, :] < counts[:, :, None]
    kernel_map = jnp.where(live_slots[:, :, None, :], gathered, NB).astype(jnp.int32)
    send_pos = []
    for drift_step, wire_step in DIRECTIONS:
        send_pos = send_pos + face_positions(drift_step, wire_step)
    send_lists = slot_of_pos[:, :, jnp.asarray(np.array(send_pos, np.int32))].astype(jnp.int32)
    return (counts, kernel_map, send_lists)


def draw_counts(key, part):
    return geometry(key)[0]


def draw_kernel_map(key, part):
    return geometry(key)[1]


def draw_send_lists(key, part):
    return geometry(key)[2]


def steps_of(stream_key, shape, cuts, low, high):
    factor_of = 1.0
    for dim, blocks in cuts:
        draws = jax.random.uniform(jax.random.fold_in(jax.random.fold_in(stream_key, 6), dim), (blocks,), jnp.float32, low / len(cuts), high / len(cuts))
        factor_of = factor_of * jnp.repeat(jnp.exp(draws), shape[dim] // blocks).reshape((-1,) + (1,) * (len(shape) - 1 - dim))
    return factor_of


def normal_values(rng, extent, width, limit, shards=(), kind=jnp.bfloat16):
    values = jax.random.normal(rng, extent, jnp.float32) * width
    if len(shards) > 0:
        values = steps_of(rng, extent, shards, -0.22, 0.18) * values
    return jnp.clip(values, min=-limit, max=limit).astype(kind)


def setup_inputs(seed: int = 0) -> dict:
    keys = jax.random.split(jax.random.key(seed), 8)
    features = normal_values(keys[0], (DRIFT_PARTS, WIRE_PARTS, NB * 64, C), 1.0, 6.0, ((0, 16), (1, 16)))
    first_weight = normal_values(keys[1], (27, C, C), (27 * C) ** -0.5, 0.109375)
    second_weight = normal_values(keys[2], (27, C, C), (27 * C) ** -0.5, 0.109375)
    cotangent = normal_values(keys[3], (DRIFT_PARTS, WIRE_PARTS, NB * 64, C), 1.0, 6.0, ((0, 16), (1, 16)))
    counts = draw_counts(jax.random.fold_in(keys[7], 71), 0)
    kernel_map = draw_kernel_map(jax.random.fold_in(keys[7], 71), 0)
    send_lists = draw_send_lists(jax.random.fold_in(keys[7], 71), 0)
    return dict(features=features, first_weight=first_weight, second_weight=second_weight, cotangent=cotangent, counts=counts, kernel_map=kernel_map, send_lists=send_lists)


DIRECTIONS = ((-1, 0), (1, 0), (0, -1), (0, 1), (-1, -1), (-1, 1), (1, -1), (1, 1))

def segment_length(drift_step, wire_step):
    return (BX if drift_step == 0 else 1) * (BW if wire_step == 0 else 1) * BZ

def segment_start(drift_step, wire_step):
    first_row = 0
    for direction in DIRECTIONS:
        if direction == (drift_step, wire_step):
            return first_row
        first_row = first_row + segment_length(direction[0], direction[1])
    return first_row

def voxel_span(step_value):
    if step_value < 0:
        return slice(3, 4)
    if step_value == 0:
        return slice(0, 4)
    return slice(0, 1)

def neighbourhood(block_table, kernel_rows):
    planes = []
    for step_x in (-1, 0, 1):
        columns = []
        for step_y in (-1, 0, 1):
            pieces = []
            for step_z in (-1, 0, 1):
                offset = 9 * (step_x + 1) + 3 * (step_y + 1) + (step_z + 1)
                sliced = block_table[:, voxel_span(step_x), voxel_span(step_y), voxel_span(step_z), :]
                pieces.append(jnp.take(sliced, kernel_rows[offset], axis=0))
            columns.append(jnp.concatenate(pieces, axis=3))
        planes.append(jnp.concatenate(columns, axis=2))
    return jnp.concatenate(planes, axis=1)

def gather_columns(window, shift_x):
    block_count = window.shape[0]
    channels = window.shape[-1]
    pieces = []
    for shift_y in range(3):
        for shift_z in range(3):
            sliced = window[:, shift_x:shift_x + 4, shift_y:shift_y + 4, shift_z:shift_z + 4, :]
            pieces.append(sliced.reshape(block_count * 64, channels))
    return jnp.concatenate(pieces, axis=1)

def convolve(window, weight):
    channels = window.shape[-1]
    summed = jnp.zeros((window.shape[0] * 64, weight.shape[2]), jnp.float32)
    for shift_x in range(3):
        stacked = gather_columns(window, shift_x)
        matrix = weight[9 * shift_x:9 * shift_x + 9].reshape(9 * channels, weight.shape[2])
        summed = summed + jnp.dot(stacked, matrix, preferred_element_type=jnp.float32)
    return summed

def weight_terms(window, grad_rows):
    groups = []
    for shift_x in range(3):
        stacked = gather_columns(window, shift_x)
        product = jnp.dot(stacked.T, grad_rows, preferred_element_type=jnp.float32)
        groups.append(product.reshape(9, window.shape[-1], grad_rows.shape[1]))
    return jnp.concatenate(groups, axis=0)

def flipped(weight):
    return jnp.transpose(weight[::-1], (0, 2, 1))

def silu_slope(pre_value):
    sigmoid_value = jax.nn.sigmoid(pre_value)
    return sigmoid_value * (1.0 + pre_value * (1.0 - sigmoid_value))

def region_table(blocks, send_lists, drift_index, wire_index):
    pieces = [blocks[drift_index, wire_index]]
    for drift_step, wire_step in DIRECTIONS:
        near_drift = drift_index + drift_step
        near_wire = wire_index + wire_step
        inside = (near_drift >= 0) & (near_drift < DRIFT_PARTS) & (near_wire >= 0) & (near_wire < WIRE_PARTS)
        clipped_drift = jnp.clip(near_drift, 0, DRIFT_PARTS - 1)
        clipped_wire = jnp.clip(near_wire, 0, WIRE_PARTS - 1)
        first_row = segment_start(-drift_step, -wire_step)
        length = segment_length(-drift_step, -wire_step)
        entries = send_lists[clipped_drift, clipped_wire, first_row:first_row + length]
        picked = jnp.take(blocks[clipped_drift, clipped_wire], entries, axis=0)
        pieces.append(jnp.where(inside, picked, jnp.zeros_like(picked)))
    return jnp.concatenate(pieces, axis=0)

def as_blocks(source):
    shaped = source.reshape(DRIFT_PARTS, WIRE_PARTS, NB, 4, 4, 4, C)
    zero_block = jnp.zeros((DRIFT_PARTS, WIRE_PARTS, 1, 4, 4, 4, C), source.dtype)
    return jnp.concatenate([shaped, zero_block], axis=2)

def reference(features, first_weight, second_weight, cotangent, counts, kernel_map, send_lists):
    slot_ids = jnp.arange(NB * 64, dtype=jnp.int32) // 64
    live_rows = (slot_ids[None, None, :] < counts[:, :, None])[..., None]
    masked_input = jnp.where(live_rows, features, jnp.zeros_like(features))
    regions = jnp.arange(DRIFT_PARTS * WIRE_PARTS, dtype=jnp.int32)

    def windows(blocks, region):
        drift_index = region // WIRE_PARTS
        wire_index = region % WIRE_PARTS
        block_table = region_table(blocks, send_lists, drift_index, wire_index)
        return neighbourhood(block_table, kernel_map[drift_index, wire_index])

    def apply_conv(source, weight):
        blocks = as_blocks(source)
        result = lax.map(lambda region: convolve(windows(blocks, region), weight), regions)
        return result.reshape(DRIFT_PARTS, WIRE_PARTS, NB * 64, C)

    def weight_sum(source, grad_field):
        blocks = as_blocks(source)
        flat_grads = grad_field.reshape(DRIFT_PARTS * WIRE_PARTS, NB * 64, C)

        def accumulate(running, region):
            return (running + weight_terms(windows(blocks, region), flat_grads[region]), None)
        summed, unused = lax.scan(accumulate, jnp.zeros((27, C, C), jnp.float32), regions)
        return summed / math.sqrt(float(VOXELS))
    first_pre = apply_conv(masked_input, first_weight)
    hidden = jnp.where(live_rows, jax.nn.silu(first_pre), 0.0).astype(jnp.bfloat16)
    second_pre = apply_conv(hidden, second_weight)
    output = jnp.where(live_rows, masked_input.astype(jnp.float32) + second_pre, 0.0).astype(jnp.bfloat16)
    grad_in = jnp.where(live_rows, cotangent, jnp.zeros_like(cotangent))
    back_hidden = apply_conv(grad_in, flipped(second_weight))
    back_pre = jnp.where(live_rows, back_hidden * silu_slope(first_pre), 0.0).astype(jnp.bfloat16)
    back_input = apply_conv(back_pre, flipped(first_weight))
    grad_features = jnp.where(live_rows, grad_in.astype(jnp.float32) + back_input, 0.0).astype(jnp.bfloat16)
    grad_second = weight_sum(hidden, grad_in)
    grad_first = weight_sum(masked_input, back_pre)
    return (output, grad_features, grad_first, grad_second)
```

```python
import functools
import math

import jax
import jax.numpy as jnp
from jax import lax
from jax.experimental import pallas as pl
from jax.experimental.pallas import tpu as pltpu
from jax.sharding import PartitionSpec as P

C = 128
PLANES = 12 * 4
ROWS = PLANES * 16
TAPS = 27
MESH = pl.DeviceIdType.MESH
NEIGHBOURS = ((-1, 0), (1, 0), (0, -1), (0, 1), (-1, -1), (-1, 1), (1, -1), (1, 1))


def place(drift, wire):
    return (drift, wire)


def greet(peers):
    barrier = pltpu.get_barrier_semaphore()
    for peer in peers:
        pl.semaphore_signal(barrier, inc=1, device_id=peer, device_id_type=MESH)
    pl.semaphore_wait(barrier, len(peers))


def halo_kernel(sizes, x_ref, y_ref, c_ref, xo_ref, yo_ref, co_ref, send_sem, recv_sem):
    drift_size, wire_size = sizes
    d = lax.axis_index("drift")
    w = lax.axis_index("wire")
    peers = [
        place(
            lax.rem(d + dd + drift_size, drift_size), lax.rem(w + ww + wire_size, wire_size)
        )
        for dd, ww in NEIGHBOURS
    ]
    greet(peers)
    copies = []
    for n, peer in enumerate(peers):
        src, dst, slot = (
            (x_ref, xo_ref, n) if n < 2 else (y_ref, yo_ref, n - 2) if n < 4 else (c_ref, co_ref, n - 4)
        )
        copy = pltpu.make_async_remote_copy(
            src_ref=src.at[slot],
            dst_ref=dst.at[slot],
            send_sem=send_sem.at[n],
            recv_sem=recv_sem.at[n],
            device_id=peer,
            device_id_type=MESH,
        )
        copy.start()
        copies.append(copy)
    for copy in copies:
        copy.wait()


def exchange(fields, sizes, ident):
    x_send = jnp.stack([fields[:, 0], fields[:, 11]])
    y_send = jnp.stack([fields[:, :, :, 1], fields[:, :, :, 12]]).reshape(2, 2 * PLANES, C)
    c_send = jnp.stack(
        [fields[:, x, :, y] for x in (0, 11) for y in (1, 12)]
    ).reshape(4, 8, C)
    vmem = pl.BlockSpec(memory_space=pltpu.VMEM)
    x_got, y_got, c_got = pl.pallas_call(
        functools.partial(halo_kernel, sizes),
        out_shape=[jax.ShapeDtypeStruct(a.shape, a.dtype) for a in (x_send, y_send, c_send)],
        in_specs=[vmem] * 3,
        out_specs=[vmem] * 3,
        scratch_shapes=[pltpu.SemaphoreType.DMA((8,)), pltpu.SemaphoreType.DMA((8,))],
        compiler_params=pltpu.CompilerParams(collective_id=ident, has_side_effects=True),
        name="halo" + str(ident),
    )(x_send, y_send, c_send)
    d = lax.axis_index("drift")
    w = lax.axis_index("wire")
    d_low, d_high = d > 0, d < sizes[0] - 1
    w_low, w_high = w > 0, w < sizes[1] - 1

    def keep(value, ok):
        return jnp.where(ok, value, jnp.zeros_like(value))

    x_low = keep(x_got[1], d_low)[:, None]
    x_high = keep(x_got[0], d_high)[:, None]
    y_got = y_got.reshape(2, 2, 12, 4, C)
    c_got = c_got.reshape(4, 2, 1, 4, C)
    y_low = jnp.concatenate(
        [keep(c_got[3], d_low & w_low), keep(y_got[1], w_low), keep(c_got[1], d_high & w_low)], axis=1
    )
    y_high = jnp.concatenate(
        [keep(c_got[2], d_low & w_high), keep(y_got[0], w_high), keep(c_got[0], d_high & w_high)], axis=1
    )
    base = jnp.concatenate([x_low, fields, x_high], axis=1)
    rows = lax.broadcasted_iota(jnp.int32, base.shape, 3)
    return jnp.where(
        rows == 0, y_low[:, :, :, None], jnp.where(rows == 13, y_high[:, :, :, None], base)
    )


def columns(source, padded, shifted, out):
    padded[...] = jnp.zeros_like(padded)
    for x in range(14):
        start = 8 + (x * 6 + 1) * 16
        padded[start : start + 64, :] = source[x].reshape(64, C).astype(jnp.float32)
    for oy in range(3):
        shifted[...] = padded[7 + oy : 7 + oy + 1344, :].astype(jnp.bfloat16).reshape(14, 96, C)
        for ox in range(3):
            for oz in range(3):
                k = 9 * ox + 3 * oy + oz
                out[:, k * C : (k + 1) * C] = shifted[
                    ox : ox + 12, oz * 16 : oz * 16 + 64, :
                ].reshape(ROWS, C)


def first_kernel(
    pad_ref, w1_ref, w2f_ref, mask_ref, hid_ref, bp_ref, g_ref,
    padded, shifted, cols_m, cols_g, hid_t, bp_t,
):
    columns(pad_ref.at[0], padded, shifted, cols_m)
    columns(pad_ref.at[1], padded, shifted, cols_g)

    def rows_step(i, carry):
        rows = pl.ds(pl.multiple_of(i * 256, 256), 256)
        pre = jnp.dot(cols_m[rows, :], w1_ref[...], preferred_element_type=jnp.float32)
        back = jnp.dot(cols_g[rows, :], w2f_ref[...], preferred_element_type=jnp.float32)
        live = mask_ref[rows, :] > 0
        gate = 1.0 / (1.0 + jnp.exp(-pre))
        hid = jnp.where(live, pre / (1.0 + jnp.exp(-pre)), 0.0)
        bp = jnp.where(live, back * (gate * (1.0 + pre * (1.0 - gate))), 0.0)
        hid_ref[rows, :] = hid.astype(jnp.bfloat16)
        bp_ref[rows, :] = bp.astype(jnp.bfloat16)
        hid_t[:, rows] = hid.T.astype(jnp.bfloat16)
        bp_t[:, rows] = bp.T.astype(jnp.bfloat16)
        return carry

    lax.fori_loop(0, ROWS // 256, rows_step, 0)

    def taps_step(j, carry):
        lanes = pl.ds(pl.multiple_of(j * 3 * C, C), 3 * C)
        one = jnp.dot(bp_t[...], cols_m[:, lanes], preferred_element_type=jnp.float32)
        two = jnp.dot(hid_t[...], cols_g[:, lanes], preferred_element_type=jnp.float32)
        for t in range(3):
            k = 3 * j + t
            part = slice(t * C, (t + 1) * C)
            g_ref[0, pl.ds(pl.multiple_of(k * C, C), C), :] = one[:, part].T
            g_ref[1, pl.ds(pl.multiple_of((26 - k) * C, C), C), :] = two[:, part]
        return carry

    lax.fori_loop(0, 9, taps_step, 0)


def second_kernel(
    pad_ref, w2_ref, w1f_ref, own_ref, out_ref, padded, shifted, cols
):
    for field, weight in ((0, w2_ref), (1, w1f_ref)):
        columns(pad_ref.at[field], padded, shifted, cols)

        def rows_step(i, carry):
            rows = pl.ds(pl.multiple_of(i * 256, 256), 256)
            value = jnp.dot(cols[rows, :], weight[...], preferred_element_type=jnp.float32)
            out_ref[field, rows, :] = (own_ref[field, rows, :].astype(jnp.float32) + value).astype(
                jnp.bfloat16
            )
            return carry

        lax.fori_loop(0, ROWS // 256, rows_step, 0)


def reduce_kernel(
    sizes, scale, g_ref, o_ref, pair_in, chip_out, chip_in, acc, wire_in, gathered,
    pair_s, pair_r, chip_s, chip_r, wire_s, wire_r, back_s, back_r, out_s, out_r, fwd_s, fwd_r,
):
    drift_size, wire_size = sizes
    chips = drift_size // 2
    chunk = TAPS * C // chips
    piece = acc.shape[0] // wire_size
    d = lax.axis_index("drift")
    w = lax.axis_index("wire")
    core = lax.rem(d, 2)
    chip = d // 2
    partner = place(d + 1 - 2 * core, w)
    chip_peers = []
    wire_peers = []
    for i in range(chips):
        chip_peers.append(lax.rem(chip + 1 + i, chips))
    for i in range(wire_size - 1):
        wire_peers.append(lax.rem(w + 1 + i, wire_size))
    chip_places = [place(2 * peer + core, w) for peer in chip_peers[:-1]]
    wire_places = [place(d, peer) for peer in wire_peers]
    greet([partner] + chip_places + wire_places)

    def send(src, dst, send_sem, recv_sem, peer):
        copy = pltpu.make_async_remote_copy(
            src_ref=src, dst_ref=dst, send_sem=send_sem, recv_sem=recv_sem,
            device_id=peer, device_id_type=MESH,
        )
        copy.start()
        return copy

    def span(index, size):
        return pl.ds(pl.multiple_of(index * size, 16), size)

    pair = []
    for i, peer in enumerate(chip_peers):
        pair.append(
            send(
                g_ref.at[1 - core, span(peer, chunk)], pair_in.at[i],
                pair_s.at[i], pair_r.at[i], partner,
            )
        )
    acc[...] = jnp.zeros_like(acc)
    ring = []
    for i, peer in enumerate(chip_peers):
        pair[i].wait_recv()
        total = g_ref[core, span(peer, chunk), :] + pair_in[i]
        if i < chips - 1:
            chip_out[i] = total.astype(jnp.bfloat16)
            ring.append(
                send(chip_out.at[i], chip_in.at[i], chip_s.at[i], chip_r.at[i], chip_places[i])
            )
        else:
            acc[0:chunk, :] = total
    for i, copy in enumerate(ring):
        copy.wait_recv()
        acc[0:chunk, :] += chip_in[i].astype(jnp.float32)
    wires = []
    for i, peer in enumerate(wire_peers):
        wires.append(
            send(
                acc.at[span(peer, piece)], wire_in.at[i], wire_s.at[i], wire_r.at[i],
                wire_places[i],
            )
        )
    own = acc[span(w, piece), :]
    for i, copy in enumerate(wires):
        copy.wait_recv()
        own = own + wire_in[i]
    gathered[span(w, piece), :] = (own * scale).astype(jnp.bfloat16)
    back = []
    for i in range(wire_size - 1):
        mine = gathered.at[span(w, piece)]
        back.append(send(mine, mine, back_s.at[i], back_r.at[i], wire_places[i]))
    for copy in back:
        copy.wait_recv()
    full = gathered.at[0:chunk]
    spot = o_ref.at[core, span(chip, chunk)]
    outs = []
    for i in range(chips - 1):
        outs.append(send(full, spot, out_s.at[i], out_r.at[i], chip_places[i]))
    forwards = [send(full, spot, fwd_s.at[chips - 1], fwd_r.at[chips - 1], partner)]
    o_ref[core, span(chip, chunk), :] = gathered[0:chunk, :]
    for i in range(chips - 1):
        outs[i].wait_recv()
        source = lax.rem(chip + 2 * chips - 1 - i, chips)
        part = o_ref.at[core, span(source, chunk)]
        forwards.append(send(part, part, fwd_s.at[i], fwd_r.at[i], partner))
    for copy in forwards:
        copy.wait_recv()
    for copy in pair + ring + wires + back + outs + forwards:
        copy.wait_send()


def reduce_all(grads, sizes, scale):
    drift_size, wire_size = sizes
    chips = drift_size // 2
    chunk = TAPS * C // chips
    piece = -(-chunk // (wire_size * 16)) * 16
    vmem = pl.BlockSpec(memory_space=pltpu.VMEM)
    dma = pltpu.SemaphoreType.DMA
    return pl.pallas_call(
        functools.partial(reduce_kernel, sizes, scale),
        out_shape=jax.ShapeDtypeStruct((2, TAPS * C, C), jnp.bfloat16),
        in_specs=[vmem],
        out_specs=vmem,
        scratch_shapes=[
            pltpu.VMEM((chips, chunk, C), jnp.float32),
            pltpu.VMEM((chips - 1, chunk, C), jnp.bfloat16),
            pltpu.VMEM((chips - 1, chunk, C), jnp.bfloat16),
            pltpu.VMEM((piece * wire_size, C), jnp.float32),
            pltpu.VMEM((wire_size - 1, piece, C), jnp.float32),
            pltpu.VMEM((piece * wire_size, C), jnp.bfloat16),
            dma((chips,)), dma((chips,)),
            dma((chips - 1,)), dma((chips - 1,)),
            dma((wire_size - 1,)), dma((wire_size - 1,)),
            dma((wire_size - 1,)), dma((wire_size - 1,)),
            dma((chips - 1,)), dma((chips - 1,)),
            dma((chips,)), dma((chips,)),
        ],
        compiler_params=pltpu.CompilerParams(collective_id=2, has_side_effects=True),
        name="reduce",
    )(grads)


def flipped(weight):
    return jnp.transpose(weight[::-1], (0, 2, 1)).reshape(TAPS * C, C)


def on_device(features, first_weight, second_weight, cotangent, counts, kernel_map, send_lists):
    sizes = (lax.axis_size("drift"), lax.axis_size("wire"))
    lists = send_lists[0, 0]
    count = counts[0, 0]
    around = jnp.stack([lists[n] for n in (0, 1, 2, 7, 10, 3, 4, 5)])
    active_around = around < 9
    centre = jnp.where(
        count > jnp.sum(active_around.astype(jnp.int32)),
        jnp.sum(active_around[:4].astype(jnp.int32)),
        9,
    )
    slots = jnp.concatenate([around[:4], centre[None], around[4:]])
    live_pos = slots < 9

    both = jnp.stack([features[0, 0], cotangent[0, 0]]).reshape(2, 9, 64, C)
    picked = jnp.take(both, jnp.minimum(slots, 8), axis=1)
    picked = jnp.where(live_pos[None, :, None, None], picked, jnp.zeros_like(picked))
    dense = picked.reshape(2, 3, 3, 4, 4, 4, C).transpose(0, 1, 3, 5, 2, 4, 6)
    dense = jnp.pad(dense.reshape(2, 12, 4, 12, C), ((0, 0), (0, 0), (0, 0), (1, 3), (0, 0)))

    mask = jnp.broadcast_to(live_pos.reshape(3, 1, 1, 3, 1, 1), (3, 4, 4, 3, 4, C))
    mask = jnp.pad(
        mask.astype(jnp.float32).reshape(12, 4, 12, C), ((0, 0), (0, 0), (1, 3), (0, 0))
    ).reshape(ROWS, C)

    vmem = pl.BlockSpec(memory_space=pltpu.VMEM)
    work = [pltpu.VMEM((1360, C), jnp.float32), pltpu.VMEM((14, 96, C), jnp.bfloat16)]
    cols = pltpu.VMEM((ROWS, TAPS * C), jnp.bfloat16)
    first_padded = exchange(dense, sizes, 0)
    hidden, back_pre, grads = pl.pallas_call(
        first_kernel,
        out_shape=[
            jax.ShapeDtypeStruct((ROWS, C), jnp.bfloat16),
            jax.ShapeDtypeStruct((ROWS, C), jnp.bfloat16),
            jax.ShapeDtypeStruct((2, TAPS * C, C), jnp.float32),
        ],
        in_specs=[vmem] * 4,
        out_specs=[vmem] * 3,
        scratch_shapes=work
        + [cols, cols, pltpu.VMEM((C, ROWS), jnp.bfloat16), pltpu.VMEM((C, ROWS), jnp.bfloat16)],
        compiler_params=pltpu.CompilerParams(vmem_limit_bytes=48 << 20),
        name="first",
    )(first_padded, first_weight.reshape(TAPS * C, C), flipped(second_weight), mask)

    second_padded = exchange(
        jnp.stack([hidden, back_pre]).reshape(2, 12, 4, 16, C), sizes, 1
    )
    summed = pl.pallas_call(
        second_kernel,
        out_shape=jax.ShapeDtypeStruct((2, ROWS, C), jnp.bfloat16),
        in_specs=[vmem] * 4,
        out_specs=vmem,
        scratch_shapes=work + [cols],
        compiler_params=pltpu.CompilerParams(vmem_limit_bytes=32 << 20),
        name="second",
    )(
        second_padded,
        second_weight.reshape(TAPS * C, C),
        flipped(first_weight),
        dense.reshape(2, ROWS, C),
    )
    scale = 1.0 / math.sqrt(float(sizes[0] * sizes[1] * 576))
    reduced = reduce_all(grads, sizes, scale)

    blocks = summed.reshape(2, 3, 4, 4, 16, C)[:, :, :, :, 1:13]
    blocks = blocks.reshape(2, 3, 4, 4, 3, 4, C).transpose(0, 1, 4, 2, 5, 3, 6)
    blocks = blocks.reshape(2, 9, 64, C)
    slot_ids = jnp.arange(9, dtype=jnp.int32)
    matches = slots[None, :] == slot_ids[:, None]
    positions = jnp.sum(jnp.where(matches, slot_ids[None, :], 0), axis=1)
    placed = jnp.take(blocks, positions, axis=1)
    placed = jnp.where((slot_ids < count)[None, :, None, None], placed, jnp.zeros_like(placed))
    placed = placed.reshape(2, 1, 1, 576, C)
    weights = reduced.astype(jnp.float32).reshape(2, TAPS, C, C)
    return placed[0], placed[1], weights[0], weights[1]


def solution(mesh):
    placed = (
        P("drift", "wire", None, None),
        P(),
        P(),
        P("drift", "wire", None, None),
        P("drift", "wire"),
        P("drift", "wire", None, None),
        P("drift", "wire", None),
    )
    return jax.shard_map(
        on_device,
        mesh=mesh,
        in_specs=placed,
        out_specs=(P("drift", "wire", None, None), P("drift", "wire", None, None), P(), P()),
        check_vma=False,
    )
```

```python
import functools
import math

import jax
import jax.numpy as jnp
import numpy as np
from jax import lax
from jax.experimental import pallas as pl
from jax.experimental.pallas import tpu as pltpu
from jax.sharding import PartitionSpec as P

C = 128
PLANES = 12 * 4
ROWS = PLANES * 16
TAPS = 27
LISTED = np.arange(16)[None, :] == np.array([0, 1, 2, 7, -1, 10, 3, 4, 5])[:, None]
AROUND = np.arange(9) != 4
BEFORE = np.arange(9) < 4
MESH = pl.DeviceIdType.MESH
NEIGHBOURS = ((-1, 0), (1, 0), (0, -1), (0, 1), (-1, -1), (-1, 1), (1, -1), (1, 1))


def place(drift, wire):
    return (drift, wire)


def greet(peers):
    barrier = pltpu.get_barrier_semaphore()
    for peer in peers:
        pl.semaphore_signal(barrier, inc=1, device_id=peer, device_id_type=MESH)
    pl.semaphore_wait(barrier, len(peers))


def halo_peers(sizes):
    d = lax.axis_index("drift")
    w = lax.axis_index("wire")
    return [
        place(lax.rem(d + dd + sizes[0], sizes[0]), lax.rem(w + ww + sizes[1], sizes[1]))
        for dd, ww in NEIGHBOURS
    ]


def halo_start(peers, sends, halos, send_sem, recv_sem):
    copies = []
    for n, peer in enumerate(peers):
        which, slot = (0, n) if n < 2 else (1, n - 2) if n < 4 else (2, n - 4)
        copy = pltpu.make_async_remote_copy(
            src_ref=sends[which].at[slot],
            dst_ref=halos[which].at[slot],
            send_sem=send_sem.at[n],
            recv_sem=recv_sem.at[n],
            device_id=peer,
            device_id_type=MESH,
        )
        copy.start()
        copies.append(copy)
    return copies


def halo_scratch():
    return [
        pltpu.VMEM((2, 2, 4, 16, C), jnp.bfloat16),
        pltpu.VMEM((2, 2 * PLANES, C), jnp.bfloat16),
        pltpu.VMEM((4, 8, C), jnp.bfloat16),
        pltpu.SemaphoreType.DMA((8,)),
        pltpu.SemaphoreType.DMA((8,)),
    ]


def faces(fields):
    x_send = jnp.stack([fields[:, 0], fields[:, 11]])
    y_send = jnp.stack([fields[:, :, :, 1], fields[:, :, :, 12]]).reshape(2, 2 * PLANES, C)
    c_send = jnp.stack(
        [fields[:, x, :, y] for x in (0, 11) for y in (1, 12)]
    ).reshape(4, 8, C)
    return x_send, y_send, c_send


def flip(weight, out):
    for k in range(TAPS):
        tap = weight[(26 - k) * C : (27 - k) * C, :].astype(jnp.float32)
        out[k * C : (k + 1) * C, :] = tap.T.astype(jnp.bfloat16)


def columns(sizes, field, own, halos, padded, edge, shifted, out):
    x_got, y_got, c_got = halos
    d = lax.axis_index("drift")
    w = lax.axis_index("wire")
    d_ok = (d > 0, d < sizes[0] - 1)
    w_ok = (w > 0, w < sizes[1] - 1)

    def keep(value, ok):
        value = value.astype(jnp.float32)
        return jnp.where(ok, value, jnp.zeros_like(value))

    padded[...] = jnp.zeros_like(padded)
    for x in range(14):
        start = 8 + (x * 6 + 1) * 16
        if x == 0:
            value = keep(x_got[1, field].reshape(64, C), d_ok[0])
        elif x == 13:
            value = keep(x_got[0, field].reshape(64, C), d_ok[1])
        else:
            value = own[field, (x - 1) * 64 : x * 64, :].astype(jnp.float32)
        padded[start : start + 64, :] = value
    for side in range(2):
        edge[0:96, :] = keep(y_got[1 - side], w_ok[side])
        edge[96:104, :] = keep(c_got[3 - side], d_ok[0] & w_ok[side])
        edge[104:112, :] = keep(c_got[1 - side], d_ok[1] & w_ok[side])
        for x in range(14):
            first = 96 if x == 0 else 104 if x == 13 else field * PLANES + (x - 1) * 4
            first = first + (field * 4 if x in (0, 13) else 0)
            start = 8 + (x * 6 + 1) * 16 + 13 * side
            padded[pl.ds(start, 4, stride=16), :] = edge[first : first + 4, :]
    for oy in range(3):
        shifted[...] = padded[7 + oy : 7 + oy + 1344, :].astype(jnp.bfloat16).reshape(14, 96, C)
        for ox in range(3):
            for oz in range(3):
                k = 9 * ox + 3 * oy + oz
                out[:, k * C : (k + 1) * C] = shifted[
                    ox : ox + 12, oz * 16 : oz * 16 + 64, :
                ].reshape(ROWS, C)


def first_kernel(
    sizes, own_ref, x_ref, y_ref, c_ref, w1_ref, w2_ref, mask_ref, mid_ref, g_ref,
    x_got, y_got, c_got, halo_s, halo_r, padded, edge, shifted, w2f, cols_m, cols_g, hid_t, bp_t,
):
    halos = (x_got, y_got, c_got)
    peers = halo_peers(sizes)
    greet(peers)
    copies = halo_start(peers, (x_ref, y_ref, c_ref), halos, halo_s, halo_r)
    flip(w2_ref, w2f)
    for copy in copies:
        copy.wait()
    columns(sizes, 0, own_ref, halos, padded, edge, shifted, cols_m)
    columns(sizes, 1, own_ref, halos, padded, edge, shifted, cols_g)

    def rows_step(i, carry):
        rows = pl.ds(pl.multiple_of(i * 256, 256), 256)
        pre = jnp.dot(cols_m[rows, :], w1_ref[...], preferred_element_type=jnp.float32)
        back = jnp.dot(cols_g[rows, :], w2f[...], preferred_element_type=jnp.float32)
        live = mask_ref[rows, :] > 0
        gate = 1.0 / (1.0 + jnp.exp(-pre))
        hid = jnp.where(live, pre / (1.0 + jnp.exp(-pre)), 0.0)
        bp = jnp.where(live, back * (gate * (1.0 + pre * (1.0 - gate))), 0.0)
        mid_ref[0, rows, :] = hid.astype(jnp.bfloat16)
        mid_ref[1, rows, :] = bp.astype(jnp.bfloat16)
        hid_t[:, rows] = hid.T.astype(jnp.bfloat16)
        bp_t[:, rows] = bp.T.astype(jnp.bfloat16)
        return carry

    lax.fori_loop(0, ROWS // 256, rows_step, 0)

    def taps_step(j, carry):
        lanes = pl.ds(pl.multiple_of(j * 3 * C, C), 3 * C)
        one = jnp.dot(bp_t[...], cols_m[:, lanes], preferred_element_type=jnp.float32)
        two = jnp.dot(hid_t[...], cols_g[:, lanes], preferred_element_type=jnp.float32)
        for t in range(3):
            k = 3 * j + t
            part = slice(t * C, (t + 1) * C)
            g_ref[0, pl.ds(pl.multiple_of(k * C, C), C), :] = one[:, part].T
            g_ref[1, pl.ds(pl.multiple_of((26 - k) * C, C), C), :] = two[:, part]
        return carry

    lax.fori_loop(0, 9, taps_step, 0)


def reduce_kernel(
    sizes, scale, mid_ref, x_ref, y_ref, c_ref, w2_ref, w1_ref, own_ref, g_ref, out_ref, o_ref,
    x_got, y_got, c_got, halo_s, halo_r, padded, edge, shifted, w1f, cols, pair_in, chip_out, chip_in, acc, wire_in, gathered,
    pair_s, pair_r, chip_s, chip_r, wire_s, wire_r, back_s, back_r, out_s, out_r, fwd_s, fwd_r,
):
    drift_size, wire_size = sizes
    chips = drift_size // 2
    chunk = TAPS * C // chips
    piece = acc.shape[0] // wire_size
    d = lax.axis_index("drift")
    w = lax.axis_index("wire")
    core = lax.rem(d, 2)
    chip = d // 2
    partner = place(d + 1 - 2 * core, w)
    chip_peers = []
    wire_peers = []
    for i in range(chips):
        chip_peers.append(lax.rem(chip + 1 + i, chips))
    for i in range(wire_size - 1):
        wire_peers.append(lax.rem(w + 1 + i, wire_size))
    chip_places = [place(2 * peer + core, w) for peer in chip_peers[:-1]]
    wire_places = [place(d, peer) for peer in wire_peers]
    halos = (x_got, y_got, c_got)
    near = halo_peers(sizes)
    greet([partner] + chip_places + wire_places + near)
    halo_copies = halo_start(near, (x_ref, y_ref, c_ref), halos, halo_s, halo_r)

    def convolve(field, weight):
        columns(sizes, field, mid_ref, halos, padded, edge, shifted, cols)

        def rows_step(i, carry):
            rows = pl.ds(pl.multiple_of(i * 256, 256), 256)
            value = jnp.dot(cols[rows, :], weight[...], preferred_element_type=jnp.float32)
            out_ref[field, rows, :] = (own_ref[field, rows, :].astype(jnp.float32) + value).astype(
                jnp.bfloat16
            )
            return carry

        lax.fori_loop(0, ROWS // 256, rows_step, 0)

    def send(src, dst, send_sem, recv_sem, peer):
        copy = pltpu.make_async_remote_copy(
            src_ref=src, dst_ref=dst, send_sem=send_sem, recv_sem=recv_sem,
            device_id=peer, device_id_type=MESH,
        )
        copy.start()
        return copy

    def span(index, size):
        return pl.ds(pl.multiple_of(index * size, 16), size)

    pair = []
    for i, peer in enumerate(chip_peers):
        pair.append(
            send(
                g_ref.at[1 - core, span(peer, chunk)], pair_in.at[i],
                pair_s.at[i], pair_r.at[i], partner,
            )
        )
    acc[...] = jnp.zeros_like(acc)
    flip(w1_ref, w1f)
    ring = []
    for i, peer in enumerate(chip_peers):
        pair[i].wait_recv()
        total = g_ref[core, span(peer, chunk), :] + pair_in[i]
        if i < chips - 1:
            chip_out[i] = total.astype(jnp.bfloat16)
            ring.append(
                send(chip_out.at[i], chip_in.at[i], chip_s.at[i], chip_r.at[i], chip_places[i])
            )
        else:
            acc[0:chunk, :] = total
    for copy in halo_copies:
        copy.wait()
    convolve(0, w2_ref)
    for i, copy in enumerate(ring):
        copy.wait_recv()
        acc[0:chunk, :] += chip_in[i].astype(jnp.float32)
    wires = []
    for i, peer in enumerate(wire_peers):
        wires.append(
            send(
                acc.at[span(peer, piece)], wire_in.at[i], wire_s.at[i], wire_r.at[i],
                wire_places[i],
            )
        )
    convolve(1, w1f)
    own = acc[span(w, piece), :]
    for i, copy in enumerate(wires):
        copy.wait_recv()
        own = own + wire_in[i]
    gathered[span(w, piece), :] = (own * scale).astype(jnp.bfloat16)
    back = []
    for i in range(wire_size - 1):
        mine = gathered.at[span(w, piece)]
        back.append(send(mine, mine, back_s.at[i], back_r.at[i], wire_places[i]))
    for copy in back:
        copy.wait_recv()
    full = gathered.at[0:chunk]
    spot = o_ref.at[core, span(chip, chunk)]
    outs = []
    for i in range(chips - 1):
        outs.append(send(full, spot, out_s.at[i], out_r.at[i], chip_places[i]))
    forwards = [send(full, spot, fwd_s.at[chips - 1], fwd_r.at[chips - 1], partner)]
    o_ref[core, span(chip, chunk), :] = gathered[0:chunk, :]
    for i in range(chips - 1):
        outs[i].wait_recv()
        source = lax.rem(chip + 2 * chips - 1 - i, chips)
        part = o_ref.at[core, span(source, chunk)]
        forwards.append(send(part, part, fwd_s.at[i], fwd_r.at[i], partner))
    for copy in forwards:
        copy.wait_recv()
    for copy in pair + ring + wires + back + outs + forwards:
        copy.wait_send()


def work_scratch():
    return [
        pltpu.VMEM((1360, C), jnp.float32),
        pltpu.VMEM((112, C), jnp.float32),
        pltpu.VMEM((14, 96, C), jnp.bfloat16),
        pltpu.VMEM((TAPS * C, C), jnp.bfloat16),
        pltpu.VMEM((ROWS, TAPS * C), jnp.bfloat16),
    ]


def first_stage(sizes, dense, first_weight, second_weight, mask):
    vmem = pl.BlockSpec(memory_space=pltpu.VMEM)
    return pl.pallas_call(
        functools.partial(first_kernel, sizes),
        out_shape=[
            jax.ShapeDtypeStruct((2, ROWS, C), jnp.bfloat16),
            jax.ShapeDtypeStruct((2, TAPS * C, C), jnp.float32),
        ],
        in_specs=[vmem] * 7,
        out_specs=[vmem] * 2,
        scratch_shapes=halo_scratch()
        + work_scratch()
        + [
            pltpu.VMEM((ROWS, TAPS * C), jnp.bfloat16),
            pltpu.VMEM((C, ROWS), jnp.bfloat16),
            pltpu.VMEM((C, ROWS), jnp.bfloat16),
        ],
        compiler_params=pltpu.CompilerParams(
            collective_id=0, has_side_effects=True, vmem_limit_bytes=48 << 20
        ),
        name="first",
    )(dense.reshape(2, ROWS, C), *faces(dense), first_weight, second_weight, mask)


def second_stage(sizes, scale, middle, first_weight, second_weight, dense, grads):
    drift_size, wire_size = sizes
    chips = drift_size // 2
    chunk = TAPS * C // chips
    piece = -(-chunk // (wire_size * 16)) * 16
    vmem = pl.BlockSpec(memory_space=pltpu.VMEM)
    dma = pltpu.SemaphoreType.DMA
    return pl.pallas_call(
        functools.partial(reduce_kernel, sizes, scale),
        out_shape=[
            jax.ShapeDtypeStruct((2, ROWS, C), jnp.bfloat16),
            jax.ShapeDtypeStruct((2, TAPS * C, C), jnp.bfloat16),
        ],
        in_specs=[vmem] * 8,
        out_specs=[vmem] * 2,
        scratch_shapes=halo_scratch()
        + work_scratch()
        + [
            pltpu.VMEM((chips, chunk, C), jnp.float32),
            pltpu.VMEM((chips - 1, chunk, C), jnp.bfloat16),
            pltpu.VMEM((chips - 1, chunk, C), jnp.bfloat16),
            pltpu.VMEM((piece * wire_size, C), jnp.float32),
            pltpu.VMEM((wire_size - 1, piece, C), jnp.float32),
            pltpu.VMEM((piece * wire_size, C), jnp.bfloat16),
            dma((chips,)), dma((chips,)),
            dma((chips - 1,)), dma((chips - 1,)),
            dma((wire_size - 1,)), dma((wire_size - 1,)),
            dma((wire_size - 1,)), dma((wire_size - 1,)),
            dma((chips - 1,)), dma((chips - 1,)),
            dma((chips,)), dma((chips,)),
        ],
        compiler_params=pltpu.CompilerParams(
            collective_id=1, has_side_effects=True, vmem_limit_bytes=48 << 20
        ),
        name="second",
    )(
        middle, *faces(middle.reshape(2, 12, 4, 16, C)), second_weight, first_weight,
        dense.reshape(2, ROWS, C), grads,
    )


def on_device(features, first_weight, second_weight, cotangent, counts, kernel_map, send_lists):
    sizes = (lax.axis_size("drift"), lax.axis_size("wire"))
    lists = send_lists[0, 0]
    count = counts[0, 0]
    spread = jnp.sum(jnp.where(LISTED, lists[None, :], 0), axis=1)
    active_around = (spread < 9) & AROUND
    centre = jnp.where(
        count > jnp.sum(active_around.astype(jnp.int32)),
        jnp.sum((active_around & BEFORE).astype(jnp.int32)),
        9,
    )
    slots = jnp.where(AROUND, spread, centre)
    live_pos = slots < 9

    both = jnp.stack([features[0, 0], cotangent[0, 0]]).reshape(2, 9, 64, C)
    picked = jnp.take(both, jnp.minimum(slots, 8), axis=1)
    picked = jnp.where(live_pos[None, :, None, None], picked, jnp.zeros_like(picked))
    dense = picked.reshape(2, 3, 3, 4, 4, 4, C).transpose(0, 1, 3, 5, 2, 4, 6)
    dense = jnp.pad(dense.reshape(2, 12, 4, 12, C), ((0, 0), (0, 0), (0, 0), (1, 3), (0, 0)))

    mask = jnp.broadcast_to(live_pos.reshape(3, 1, 1, 3, 1, 1), (3, 4, 4, 3, 4, C))
    mask = jnp.pad(
        mask.astype(jnp.float32).reshape(12, 4, 12, C), ((0, 0), (0, 0), (1, 3), (0, 0))
    ).reshape(ROWS, C)

    first_rows = first_weight.reshape(TAPS * C, C)
    second_rows = second_weight.reshape(TAPS * C, C)
    middle, grads = first_stage(sizes, dense, first_rows, second_rows, mask)
    scale = 1.0 / math.sqrt(float(sizes[0] * sizes[1] * 576))
    summed, reduced = second_stage(
        sizes, scale, middle, first_rows, second_rows, dense, grads
    )

    blocks = summed.reshape(2, 3, 4, 4, 16, C)[:, :, :, :, 1:13]
    blocks = blocks.reshape(2, 3, 4, 4, 3, 4, C).transpose(0, 1, 4, 2, 5, 3, 6)
    blocks = blocks.reshape(2, 9, 64, C)
    slot_ids = jnp.arange(9, dtype=jnp.int32)
    matches = slots[None, :] == slot_ids[:, None]
    positions = jnp.sum(jnp.where(matches, slot_ids[None, :], 0), axis=1)
    placed = jnp.take(blocks, positions, axis=1)
    placed = jnp.where((slot_ids < count)[None, :, None, None], placed, jnp.zeros_like(placed))
    placed = placed.reshape(2, 1, 1, 576, C)
    weights = reduced.astype(jnp.float32).reshape(2, TAPS, C, C)
    return placed[0], placed[1], weights[0], weights[1]


def solution(mesh):
    placed = (
        P("drift", "wire", None, None),
        P(),
        P(),
        P("drift", "wire", None, None),
        P("drift", "wire"),
        P("drift", "wire", None, None),
        P("drift", "wire", None),
    )
    return jax.shard_map(
        on_device,
        mesh=mesh,
        in_specs=placed,
        out_specs=(P("drift", "wire", None, None), P("drift", "wire", None, None), P(), P()),
        check_vma=False,
    )
```

```python
import functools
import math

import jax
import jax.numpy as jnp
import numpy as np
from jax import lax
from jax.experimental import pallas as pl
from jax.experimental.pallas import tpu as pltpu
from jax.sharding import PartitionSpec as P

C = 128
PLANES = 12 * 4
ROWS = PLANES * 16
TAPS = 27
LISTED = np.arange(16)[None, :] == np.array([0, 1, 2, 7, -1, 10, 3, 4, 5])[:, None]
AROUND = np.arange(9) != 4
BEFORE = np.arange(9) < 4
MESH = pl.DeviceIdType.MESH
NEIGHBOURS = ((-1, 0), (1, 0), (0, -1), (0, 1), (-1, -1), (-1, 1), (1, -1), (1, 1))


def place(drift, wire):
    return (drift, wire)


def greet(peers):
    barrier = pltpu.get_barrier_semaphore()
    for peer in peers:
        pl.semaphore_signal(barrier, inc=1, device_id=peer, device_id_type=MESH)
    pl.semaphore_wait(barrier, len(peers))


def halo_peers(sizes):
    d = lax.axis_index("drift")
    w = lax.axis_index("wire")
    return [
        place(lax.rem(d + dd + sizes[0], sizes[0]), lax.rem(w + ww + sizes[1], sizes[1]))
        for dd, ww in NEIGHBOURS
    ]


def halo_start(peers, sends, halos, send_sem, recv_sem):
    copies = []
    for n, peer in enumerate(peers):
        which, slot = (0, n) if n < 2 else (1, n - 2) if n < 4 else (2, n - 4)
        copy = pltpu.make_async_remote_copy(
            src_ref=sends[which][slot],
            dst_ref=halos[which].at[slot],
            send_sem=send_sem.at[n],
            recv_sem=recv_sem.at[n],
            device_id=peer,
            device_id_type=MESH,
        )
        copy.start()
        copies.append(copy)
    return copies


def halo_scratch():
    return [
        pltpu.VMEM((2, 2, 64, C), jnp.bfloat16),
        pltpu.VMEM((2, 2 * PLANES, C), jnp.bfloat16),
        pltpu.VMEM((4, 8, C), jnp.bfloat16),
        pltpu.SemaphoreType.DMA((8,)),
        pltpu.SemaphoreType.DMA((8,)),
    ]


def faces(fields):
    x_send = jnp.stack([fields[:, 0], fields[:, 11]]).reshape(2, 2, 64, C)
    y_send = jnp.stack([fields[:, :, :, 1], fields[:, :, :, 12]]).reshape(2, 2 * PLANES, C)
    c_send = jnp.stack(
        [fields[:, x, :, y] for x in (0, 11) for y in (1, 12)]
    ).reshape(4, 8, C)
    return x_send, y_send, c_send


def flip(weight, out):
    for k in range(TAPS):
        tap = weight[(26 - k) * C : (27 - k) * C, :].astype(jnp.float32)
        out[k * C : (k + 1) * C, :] = tap.T.astype(jnp.bfloat16)


def columns(sizes, field, own, halos, padded, edge, shifted, out):
    x_got, y_got, c_got = halos
    d = lax.axis_index("drift")
    w = lax.axis_index("wire")
    d_ok = (d > 0, d < sizes[0] - 1)
    w_ok = (w > 0, w < sizes[1] - 1)

    def keep(value, ok):
        value = value.astype(jnp.float32)
        return jnp.where(ok, value, jnp.zeros_like(value))

    padded[...] = jnp.zeros_like(padded)
    for x in range(14):
        start = 8 + (x * 6 + 1) * 16
        if x == 0:
            value = keep(x_got[1, field], d_ok[0])
        elif x == 13:
            value = keep(x_got[0, field], d_ok[1])
        else:
            value = own[field, (x - 1) * 64 : x * 64, :].astype(jnp.float32)
        padded[start : start + 64, :] = value
    for side in range(2):
        edge[0:96, :] = keep(y_got[1 - side], w_ok[side])
        edge[96:104, :] = keep(c_got[3 - side], d_ok[0] & w_ok[side])
        edge[104:112, :] = keep(c_got[1 - side], d_ok[1] & w_ok[side])
        for x in range(14):
            first = 96 if x == 0 else 104 if x == 13 else field * PLANES + (x - 1) * 4
            first = first + (field * 4 if x in (0, 13) else 0)
            start = 8 + (x * 6 + 1) * 16 + 13 * side
            padded[pl.ds(start, 4, stride=16), :] = edge[first : first + 4, :]
    for oy in range(3):
        shifted[...] = padded[7 + oy : 7 + oy + 1344, :].astype(jnp.bfloat16).reshape(14, 96, C)
        for ox in range(3):
            for oz in range(3):
                k = 9 * ox + 3 * oy + oz
                out[:, k * C : (k + 1) * C] = shifted[
                    ox : ox + 12, oz * 16 : oz * 16 + 64, :
                ].reshape(ROWS, C)


def kernel(
    sizes, scale, own_ref, x_ref, y_ref, c_ref, w1_ref, w2_ref, mask_ref, out_ref, o_ref,
    x_got, y_got, c_got, halo_s, halo_r, x_got2, y_got2, c_got2, halo_s2, halo_r2,
    padded, edge, shifted, w1f, cols_m, w2f, cols_g, hid_t, bp_t, mid, wide, y_out, corner, c_out,
    grads, pair_in, chip_out, chip_in, acc, wire_in, gathered,
    pair_s, pair_r, chip_s, chip_r, wire_s, wire_r, back_s, back_r, out_s, out_r, fwd_s, fwd_r,
):
    drift_size, wire_size = sizes
    chips = drift_size // 2
    chunk = TAPS * C // chips
    halves = halves_of(chunk)
    piece = wire_in.shape[2]
    d = lax.axis_index("drift")
    w = lax.axis_index("wire")
    core = lax.rem(d, 2)
    chip = d // 2
    partner = place(d + 1 - 2 * core, w)
    chip_peers = [lax.rem(chip + 1 + i, chips) for i in range(chips)]
    wire_peers = [lax.rem(w + 1 + i, wire_size) for i in range(wire_size - 1)]
    chip_places = [place(2 * peer + core, w) for peer in chip_peers[:-1]]
    wire_places = [place(d, peer) for peer in wire_peers]
    near = halo_peers(sizes)
    greet([partner] + chip_places + wire_places + near)

    def send(src, dst, send_sem, recv_sem, peer):
        copy = pltpu.make_async_remote_copy(
            src_ref=src, dst_ref=dst, send_sem=send_sem, recv_sem=recv_sem,
            device_id=peer, device_id_type=MESH,
        )
        copy.start()
        return copy

    def rows_at(start, size):
        return pl.ds(pl.multiple_of(start, 16), size)

    halos = (x_got, y_got, c_got)
    first_halo = halo_start(
        near,
        ([x_ref.at[n] for n in range(2)], [y_ref.at[n] for n in range(2)],
         [c_ref.at[n] for n in range(4)]),
        halos, halo_s, halo_r,
    )
    flip(w2_ref, w2f)
    flip(w1_ref, w1f)
    acc[...] = jnp.zeros_like(acc)
    for copy in first_halo:
        copy.wait()
    columns(sizes, 0, own_ref, halos, padded, edge, shifted, cols_m)
    columns(sizes, 1, own_ref, halos, padded, edge, shifted, cols_g)

    def rows_step(i, carry):
        rows = pl.ds(pl.multiple_of(i * 256, 256), 256)
        pre = jnp.dot(cols_m[rows, :], w1_ref[...], preferred_element_type=jnp.float32)
        back = jnp.dot(cols_g[rows, :], w2f[...], preferred_element_type=jnp.float32)
        live = mask_ref[rows, :] > 0
        gate = 1.0 / (1.0 + jnp.exp(-pre))
        hid = jnp.where(live, pre / (1.0 + jnp.exp(-pre)), 0.0)
        bp = jnp.where(live, back * (gate * (1.0 + pre * (1.0 - gate))), 0.0)
        mid[0, rows, :] = hid.astype(jnp.bfloat16)
        mid[1, rows, :] = bp.astype(jnp.bfloat16)
        wide[0, rows, :] = hid
        wide[1, rows, :] = bp
        hid_t[:, rows] = hid.T.astype(jnp.bfloat16)
        bp_t[:, rows] = bp.T.astype(jnp.bfloat16)
        return carry

    lax.fori_loop(0, ROWS // 256, rows_step, 0)

    for side in range(2):
        for field in range(2):
            face = wide[field, pl.ds(1 + 11 * side, PLANES, stride=16), :]
            y_out[side, field * PLANES : (field + 1) * PLANES, :] = face.astype(jnp.bfloat16)
            corner[side, field * 4 : field * 4 + 4, :] = wide[
                field, pl.ds(1 + 11 * side, 4, stride=16), :
            ]
            corner[2 + side, field * 4 : field * 4 + 4, :] = wide[
                field, pl.ds(704 + 1 + 11 * side, 4, stride=16), :
            ]
    c_out[...] = corner[...].astype(jnp.bfloat16)
    halos2 = (x_got2, y_got2, c_got2)
    second_halo = halo_start(
        near,
        ([mid.at[:, 0:64], mid.at[:, 704:768]], [y_out.at[n] for n in range(2)],
         [c_out.at[n] for n in range(4)]),
        halos2, halo_s2, halo_r2,
    )

    def taps_step(j, carry):
        lanes = pl.ds(pl.multiple_of(j * 3 * C, C), 3 * C)
        one = jnp.dot(bp_t[...], cols_m[:, lanes], preferred_element_type=jnp.float32)
        two = jnp.dot(hid_t[...], cols_g[:, lanes], preferred_element_type=jnp.float32)
        for t in range(3):
            k = 3 * j + t
            part = slice(t * C, (t + 1) * C)
            grads[0, pl.ds(pl.multiple_of(k * C, C), C), :] = one[:, part].T
            grads[1, pl.ds(pl.multiple_of((26 - k) * C, C), C), :] = two[:, part]
        return carry

    pair = []
    for third in range(3):
        lax.fori_loop(3 * third, 3 * third + 3, taps_step, 0)
        part = rows_at(9 * C * (core * third + (1 - core) * (2 - third)), 9 * C)
        pair.append(
            send(
                grads.at[1 - core, part], pair_in.at[part],
                pair_s.at[third], pair_r.at[third], partner,
            )
        )

    for copy in second_halo:
        copy.wait()
    columns(sizes, 0, mid, halos2, padded, edge, shifted, cols_m)
    for copy in pair:
        copy.wait_recv()

    def convolve(field, weight, cols):
        def step(i, carry):
            rows = pl.ds(pl.multiple_of(i * 256, 256), 256)
            value = jnp.dot(cols[rows, :], weight[...], preferred_element_type=jnp.float32)
            out_ref[field, rows, :] = (own_ref[field, rows, :].astype(jnp.float32) + value).astype(
                jnp.bfloat16
            )
            return carry

        lax.fori_loop(0, ROWS // 256, step, 0)

    ring = ([], [])
    for h, (start, size) in enumerate(halves):
        for i, peer in enumerate(chip_peers):
            rows = rows_at(peer * chunk + start, size)
            total = grads[core, rows, :] + pair_in[rows, :]
            if i < chips - 1:
                chip_out[i, start : start + size, :] = total.astype(jnp.bfloat16)
                part = (i, slice(start, start + size))
                ring[h].append(
                    send(
                        chip_out.at[part], chip_in.at[part],
                        chip_s.at[h, i], chip_r.at[h, i], chip_places[i],
                    )
                )
            else:
                acc[h, 0:size, :] = total

    def to_wire(h):
        size = halves[h][1]
        for i, copy in enumerate(ring[h]):
            copy.wait_recv()
            start = halves[h][0]
            acc[h, 0:size, :] += chip_in[i, start : start + size, :].astype(jnp.float32)
        return [
            send(
                acc.at[h, rows_at(peer * piece, piece)], wire_in.at[h, i],
                wire_s.at[h, i], wire_r.at[h, i], wire_places[i],
            )
            for i, peer in enumerate(wire_peers)
        ]

    def from_wire(h, wires):
        own = acc[h, rows_at(w * piece, piece), :]
        for i, copy in enumerate(wires):
            copy.wait_recv()
            own = own + wire_in[h, i]
        mine = rows_at(w * piece, piece)
        gathered[h, mine, :] = (own * scale).astype(jnp.bfloat16)
        return [
            send(
                gathered.at[h, mine], gathered.at[h, mine],
                back_s.at[h, i], back_r.at[h, i], wire_places[i],
            )
            for i in range(wire_size - 1)
        ]

    def to_chips(h, back):
        for copy in back:
            copy.wait_recv()
        start, size = halves[h]
        full = gathered.at[h, 0:size]
        rows = rows_at(chip * chunk + start, size)
        spot = o_ref.at[core, rows]
        sent = [
            send(full, spot, out_s.at[h, i], out_r.at[h, i], chip_places[i])
            for i in range(chips - 1)
        ]
        ahead = send(full, spot, fwd_s.at[h, chips - 1], fwd_r.at[h, chips - 1], partner)
        o_ref[core, rows, :] = gathered[h, 0:size, :]
        return sent, [ahead]

    convolve(0, w2_ref, cols_m)
    wires0 = to_wire(0)
    columns(sizes, 1, mid, halos2, padded, edge, shifted, cols_g)
    convolve(1, w1f, cols_g)
    wires1 = to_wire(1)
    back0 = from_wire(0, wires0)
    back1 = from_wire(1, wires1)
    outs0, forwards0 = to_chips(0, back0)
    outs1, forwards1 = to_chips(1, back1)
    forwards = forwards0 + forwards1
    for h, outs in enumerate((outs0, outs1)):
        start, size = halves[h]
        for i in range(chips - 1):
            outs[i].wait_recv()
            source = lax.rem(chip + 2 * chips - 1 - i, chips)
            part = o_ref.at[core, rows_at(source * chunk + start, size)]
            forwards.append(send(part, part, fwd_s.at[h, i], fwd_r.at[h, i], partner))
    for copy in forwards:
        copy.wait_recv()
    sent = pair + ring[0] + ring[1] + wires0 + wires1 + back0 + back1 + outs0 + outs1 + forwards
    for copy in sent:
        copy.wait_send()


def halves_of(chunk):
    first = (chunk // 16 + 1) // 2 * 16
    return ((0, first), (first, chunk - first))


def work_scratch():
    return [
        pltpu.VMEM((1360, C), jnp.float32),
        pltpu.VMEM((112, C), jnp.float32),
        pltpu.VMEM((14, 96, C), jnp.bfloat16),
        pltpu.VMEM((TAPS * C, C), jnp.bfloat16),
        pltpu.VMEM((ROWS, TAPS * C), jnp.bfloat16),
    ]


def run(sizes, scale, first_weight, second_weight, dense, mask):
    drift_size, wire_size = sizes
    chips = drift_size // 2
    chunk = TAPS * C // chips
    piece = -(-halves_of(chunk)[0][1] // (wire_size * 16)) * 16
    vmem = pl.BlockSpec(memory_space=pltpu.VMEM)
    dma = pltpu.SemaphoreType.DMA
    return pl.pallas_call(
        functools.partial(kernel, sizes, scale),
        out_shape=[
            jax.ShapeDtypeStruct((2, ROWS, C), jnp.bfloat16),
            jax.ShapeDtypeStruct((2, TAPS * C, C), jnp.bfloat16),
        ],
        in_specs=[vmem] * 7,
        out_specs=[vmem] * 2,
        scratch_shapes=halo_scratch()
        + halo_scratch()
        + work_scratch()
        + [
            pltpu.VMEM((TAPS * C, C), jnp.bfloat16),
            pltpu.VMEM((ROWS, TAPS * C), jnp.bfloat16),
            pltpu.VMEM((C, ROWS), jnp.bfloat16),
            pltpu.VMEM((C, ROWS), jnp.bfloat16),
            pltpu.VMEM((2, ROWS, C), jnp.bfloat16),
            pltpu.VMEM((2, ROWS, C), jnp.float32),
            pltpu.VMEM((2, 2 * PLANES, C), jnp.bfloat16),
            pltpu.VMEM((4, 8, C), jnp.float32),
            pltpu.VMEM((4, 8, C), jnp.bfloat16),
            pltpu.VMEM((2, TAPS * C, C), jnp.float32),
            pltpu.VMEM((TAPS * C, C), jnp.float32),
            pltpu.VMEM((chips - 1, chunk, C), jnp.bfloat16),
            pltpu.VMEM((chips - 1, chunk, C), jnp.bfloat16),
            pltpu.VMEM((2, piece * wire_size, C), jnp.float32),
            pltpu.VMEM((2, wire_size - 1, piece, C), jnp.float32),
            pltpu.VMEM((2, piece * wire_size, C), jnp.bfloat16),
            dma((3,)), dma((3,)),
            dma((2, chips - 1)), dma((2, chips - 1)),
            dma((2, wire_size - 1)), dma((2, wire_size - 1)),
            dma((2, wire_size - 1)), dma((2, wire_size - 1)),
            dma((2, chips - 1)), dma((2, chips - 1)),
            dma((2, chips)), dma((2, chips)),
        ],
        compiler_params=pltpu.CompilerParams(
            collective_id=0, has_side_effects=True, vmem_limit_bytes=52 << 20
        ),
        name="layers",
    )(dense.reshape(2, ROWS, C), *faces(dense), first_weight, second_weight, mask)


def on_device(features, first_weight, second_weight, cotangent, counts, kernel_map, send_lists):
    sizes = (lax.axis_size("drift"), lax.axis_size("wire"))
    lists = send_lists[0, 0]
    count = counts[0, 0]
    spread = jnp.sum(jnp.where(LISTED, lists[None, :], 0), axis=1)
    active_around = (spread < 9) & AROUND
    centre = jnp.where(
        count > jnp.sum(active_around.astype(jnp.int32)),
        jnp.sum((active_around & BEFORE).astype(jnp.int32)),
        9,
    )
    slots = jnp.where(AROUND, spread, centre)
    live_pos = slots < 9

    both = jnp.stack([features[0, 0], cotangent[0, 0]]).reshape(2, 9, 64, C)
    picked = jnp.take(both, jnp.minimum(slots, 8), axis=1)
    picked = jnp.where(live_pos[None, :, None, None], picked, jnp.zeros_like(picked))
    dense = picked.reshape(2, 3, 3, 4, 4, 4, C).transpose(0, 1, 3, 5, 2, 4, 6)
    dense = jnp.pad(dense.reshape(2, 12, 4, 12, C), ((0, 0), (0, 0), (0, 0), (1, 3), (0, 0)))

    mask = jnp.broadcast_to(live_pos.reshape(3, 1, 1, 3, 1, 1), (3, 4, 4, 3, 4, C))
    mask = jnp.pad(
        mask.astype(jnp.float32).reshape(12, 4, 12, C), ((0, 0), (0, 0), (1, 3), (0, 0))
    ).reshape(ROWS, C)

    first_rows = first_weight.reshape(TAPS * C, C)
    second_rows = second_weight.reshape(TAPS * C, C)
    scale = 1.0 / math.sqrt(float(sizes[0] * sizes[1] * 576))
    summed, reduced = run(sizes, scale, first_rows, second_rows, dense, mask)

    blocks = summed.reshape(2, 3, 4, 4, 16, C)[:, :, :, :, 1:13]
    blocks = blocks.reshape(2, 3, 4, 4, 3, 4, C).transpose(0, 1, 4, 2, 5, 3, 6)
    blocks = blocks.reshape(2, 9, 64, C)
    slot_ids = jnp.arange(9, dtype=jnp.int32)
    matches = slots[None, :] == slot_ids[:, None]
    positions = jnp.sum(jnp.where(matches, slot_ids[None, :], 0), axis=1)
    placed = jnp.take(blocks, positions, axis=1)
    placed = jnp.where((slot_ids < count)[None, :, None, None], placed, jnp.zeros_like(placed))
    placed = placed.reshape(2, 1, 1, 576, C)
    weights = reduced.astype(jnp.float32).reshape(2, TAPS, C, C)
    return placed[0], placed[1], weights[0], weights[1]


def solution(mesh):
    placed = (
        P("drift", "wire", None, None),
        P(),
        P(),
        P("drift", "wire", None, None),
        P("drift", "wire"),
        P("drift", "wire", None, None),
        P("drift", "wire", None),
    )
    return jax.shard_map(
        on_device,
        mesh=mesh,
        in_specs=placed,
        out_specs=(P("drift", "wire", None, None), P("drift", "wire", None, None), P(), P()),
        check_vma=False,
    )
```

```python
import functools
import math

import jax
import jax.numpy as jnp
import numpy as np
from jax import lax
from jax.experimental import pallas as pl
from jax.experimental.pallas import tpu as pltpu
from jax.sharding import PartitionSpec as P

C = 128
PLANES = 12 * 4
ROWS = PLANES * 16
TAPS = 27
LISTED = np.arange(16)[None, :] == np.array([0, 1, 2, 7, -1, 10, 3, 4, 5])[:, None]
AROUND = np.arange(9) != 4
BEFORE = np.arange(9) < 4
MESH = pl.DeviceIdType.MESH
RELATIVE = ((0, 2), (1, 2), (0, 1), (0, 3), (1, 1), (1, 3), (1, 0), (0, 0))
NEIGHBOURS = ((-1, 0), (1, 0), (0, -1), (0, 1), (-1, -1), (-1, 1), (1, -1), (1, 1))


def place(drift, wire):
    return (drift, wire)


def greet(peers):
    barrier = pltpu.get_barrier_semaphore()
    for peer in peers:
        pl.semaphore_signal(barrier, inc=1, device_id=peer, device_id_type=MESH)
    pl.semaphore_wait(barrier, len(peers))


def halo_peers(sizes):
    d = lax.axis_index("drift")
    w = lax.axis_index("wire")
    return [
        place(lax.rem(d + dd + sizes[0], sizes[0]), lax.rem(w + ww + sizes[1], sizes[1]))
        for dd, ww in NEIGHBOURS
    ]


def halo_start(peers, sends, halos, send_sem, recv_sem):
    copies = []
    for n, peer in enumerate(peers):
        which, slot = (0, n) if n < 2 else (1, n - 2) if n < 4 else (2, n - 4)
        copy = pltpu.make_async_remote_copy(
            src_ref=sends[which][slot],
            dst_ref=halos[which].at[slot],
            send_sem=send_sem.at[n],
            recv_sem=recv_sem.at[n],
            device_id=peer,
            device_id_type=MESH,
        )
        copy.start()
        copies.append(copy)
    return copies


def halo_scratch():
    return [
        pltpu.VMEM((2, 2, 64, C), jnp.bfloat16),
        pltpu.VMEM((2, 2 * PLANES, C), jnp.bfloat16),
        pltpu.VMEM((4, 8, C), jnp.bfloat16),
        pltpu.SemaphoreType.DMA((8,)),
        pltpu.SemaphoreType.DMA((8,)),
    ]


def faces(fields):
    x_send = jnp.stack([fields[:, 0], fields[:, 11]]).reshape(2, 2, 64, C)
    y_send = jnp.stack([fields[:, :, :, 1], fields[:, :, :, 12]]).reshape(2, 2 * PLANES, C)
    c_send = jnp.stack(
        [fields[:, x, :, y] for x in (0, 11) for y in (1, 12)]
    ).reshape(4, 8, C)
    return x_send, y_send, c_send


def flip(weight, out):
    for k in range(TAPS):
        tap = weight[(26 - k) * C : (27 - k) * C, :].astype(jnp.float32)
        out[k * C : (k + 1) * C, :] = tap.T.astype(jnp.bfloat16)


def columns(sizes, field, own, halos, padded, edge, shifted, out):
    x_got, y_got, c_got = halos
    d = lax.axis_index("drift")
    w = lax.axis_index("wire")
    d_ok = (d > 0, d < sizes[0] - 1)
    w_ok = (w > 0, w < sizes[1] - 1)

    def keep(value, ok):
        value = value.astype(jnp.float32)
        return jnp.where(ok, value, jnp.zeros_like(value))

    padded[...] = jnp.zeros_like(padded)
    for x in range(14):
        start = 8 + (x * 6 + 1) * 16
        if x == 0:
            value = keep(x_got[1, field], d_ok[0])
        elif x == 13:
            value = keep(x_got[0, field], d_ok[1])
        else:
            value = own[field, (x - 1) * 64 : x * 64, :].astype(jnp.float32)
        padded[start : start + 64, :] = value
    for side in range(2):
        edge[0:96, :] = keep(y_got[1 - side], w_ok[side])
        edge[96:104, :] = keep(c_got[3 - side], d_ok[0] & w_ok[side])
        edge[104:112, :] = keep(c_got[1 - side], d_ok[1] & w_ok[side])
        for x in range(14):
            first = 96 if x == 0 else 104 if x == 13 else field * PLANES + (x - 1) * 4
            first = first + (field * 4 if x in (0, 13) else 0)
            start = 8 + (x * 6 + 1) * 16 + 13 * side
            padded[pl.ds(start, 4, stride=16), :] = edge[first : first + 4, :]
    for oy in range(3):
        shifted[...] = padded[7 + oy : 7 + oy + 1344, :].astype(jnp.bfloat16).reshape(14, 96, C)
        for ox in range(3):
            for oz in range(3):
                k = 9 * ox + 3 * oy + oz
                out[:, k * C : (k + 1) * C] = shifted[
                    ox : ox + 12, oz * 16 : oz * 16 + 64, :
                ].reshape(ROWS, C)


def kernel(
    sizes, scale, own_ref, x_ref, y_ref, c_ref, w1_ref, w2_ref, mask_ref, out_ref, o_ref,
    x_got, y_got, c_got, halo_s, halo_r, x_got2, y_got2, c_got2, halo_s2, halo_r2,
    padded, edge, shifted, w1f, cols_m, w2f, cols_g, hid_t, bp_t, mid, wide, y_out, corner, c_out,
    grads, pair_in, chip_out, chip_in, relay_in, acc, wire_in, gathered,
    pair_s, pair_r, chip_s, chip_r, relay_s, relay_r, wire_s, wire_r, back_s, back_r, out_s, out_r, fwd_s, fwd_r,
):
    drift_size, wire_size = sizes
    chips = drift_size // 2
    chunk = TAPS * C // chips
    halves = halves_of(chunk)
    piece = wire_in.shape[2]
    d = lax.axis_index("drift")
    w = lax.axis_index("wire")
    core = lax.rem(d, 2)
    chip = d // 2
    partner = place(d + 1 - 2 * core, w)
    chip_x, chip_y = chip // 4, lax.rem(chip, 4)

    def chip_at(dx, dy):
        column = 1 - chip_x if dx else chip_x
        return column * 4 + lax.rem(chip_y + dy, 4)

    def place_at(dx, dy):
        return place(2 * chip_at(dx, dy) + core, w)

    chip_peers = [chip_at(dx, dy) for dx, dy in RELATIVE]
    wire_peers = [lax.rem(w + 1 + i, wire_size) for i in range(wire_size - 1)]
    chip_places = [place(2 * peer + core, w) for peer in chip_peers[:-1]]
    wire_places = [place(d, peer) for peer in wire_peers]
    near = halo_peers(sizes)
    greet([partner] + chip_places + wire_places + near)

    def send(src, dst, send_sem, recv_sem, peer):
        copy = pltpu.make_async_remote_copy(
            src_ref=src, dst_ref=dst, send_sem=send_sem, recv_sem=recv_sem,
            device_id=peer, device_id_type=MESH,
        )
        copy.start()
        return copy

    def rows_at(start, size):
        return pl.ds(pl.multiple_of(start, 16), size)

    halos = (x_got, y_got, c_got)
    first_halo = halo_start(
        near,
        ([x_ref.at[n] for n in range(2)], [y_ref.at[n] for n in range(2)],
         [c_ref.at[n] for n in range(4)]),
        halos, halo_s, halo_r,
    )
    flip(w2_ref, w2f)
    flip(w1_ref, w1f)
    acc[...] = jnp.zeros_like(acc)
    for copy in first_halo:
        copy.wait()
    columns(sizes, 0, own_ref, halos, padded, edge, shifted, cols_m)
    columns(sizes, 1, own_ref, halos, padded, edge, shifted, cols_g)

    def rows_step(i, carry):
        rows = pl.ds(pl.multiple_of(i * 256, 256), 256)
        pre = jnp.dot(cols_m[rows, :], w1_ref[...], preferred_element_type=jnp.float32)
        back = jnp.dot(cols_g[rows, :], w2f[...], preferred_element_type=jnp.float32)
        live = mask_ref[rows, :] > 0
        gate = 1.0 / (1.0 + jnp.exp(-pre))
        hid = jnp.where(live, pre / (1.0 + jnp.exp(-pre)), 0.0)
        bp = jnp.where(live, back * (gate * (1.0 + pre * (1.0 - gate))), 0.0)
        mid[0, rows, :] = hid.astype(jnp.bfloat16)
        mid[1, rows, :] = bp.astype(jnp.bfloat16)
        wide[0, rows, :] = hid
        wide[1, rows, :] = bp
        hid_t[:, rows] = hid.T.astype(jnp.bfloat16)
        bp_t[:, rows] = bp.T.astype(jnp.bfloat16)
        return carry

    lax.fori_loop(0, ROWS // 256, rows_step, 0)

    for side in range(2):
        for field in range(2):
            face = wide[field, pl.ds(1 + 11 * side, PLANES, stride=16), :]
            y_out[side, field * PLANES : (field + 1) * PLANES, :] = face.astype(jnp.bfloat16)
            corner[side, field * 4 : field * 4 + 4, :] = wide[
                field, pl.ds(1 + 11 * side, 4, stride=16), :
            ]
            corner[2 + side, field * 4 : field * 4 + 4, :] = wide[
                field, pl.ds(704 + 1 + 11 * side, 4, stride=16), :
            ]
    c_out[...] = corner[...].astype(jnp.bfloat16)
    halos2 = (x_got2, y_got2, c_got2)
    second_halo = halo_start(
        near,
        ([mid.at[:, 0:64], mid.at[:, 704:768]], [y_out.at[n] for n in range(2)],
         [c_out.at[n] for n in range(4)]),
        halos2, halo_s2, halo_r2,
    )

    def taps_step(j, carry):
        lanes = pl.ds(pl.multiple_of(j * 3 * C, C), 3 * C)
        one = jnp.dot(bp_t[...], cols_m[:, lanes], preferred_element_type=jnp.float32)
        two = jnp.dot(hid_t[...], cols_g[:, lanes], preferred_element_type=jnp.float32)
        for t in range(3):
            k = 3 * j + t
            part = slice(t * C, (t + 1) * C)
            grads[0, pl.ds(pl.multiple_of(k * C, C), C), :] = one[:, part].T
            grads[1, pl.ds(pl.multiple_of((26 - k) * C, C), C), :] = two[:, part]
        return carry

    pair = []
    for third in range(3):
        lax.fori_loop(3 * third, 3 * third + 3, taps_step, 0)
        part = rows_at(9 * C * (core * third + (1 - core) * (2 - third)), 9 * C)
        pair.append(
            send(
                grads.at[1 - core, part], pair_in.at[part],
                pair_s.at[third], pair_r.at[third], partner,
            )
        )

    for copy in second_halo:
        copy.wait()
    columns(sizes, 0, mid, halos2, padded, edge, shifted, cols_m)
    for copy in pair:
        copy.wait_recv()

    def convolve(field, weight, cols):
        def step(i, carry):
            rows = pl.ds(pl.multiple_of(i * 256, 256), 256)
            value = jnp.dot(cols[rows, :], weight[...], preferred_element_type=jnp.float32)
            out_ref[field, rows, :] = (own_ref[field, rows, :].astype(jnp.float32) + value).astype(
                jnp.bfloat16
            )
            return carry

        lax.fori_loop(0, ROWS // 256, step, 0)

    ring = ([], [])
    hops = ([], [])
    for h, (start, size) in enumerate(halves):
        for i, peer in enumerate(chip_peers):
            rows = rows_at(peer * chunk + start, size)
            total = grads[core, rows, :] + pair_in[rows, :]
            if i < chips - 1:
                chip_out[i, start : start + size, :] = total.astype(jnp.bfloat16)
                part = (i, slice(start, start + size))
                if i < 2:
                    hops[h].append(
                        send(
                            chip_out.at[part], relay_in.at[part],
                            chip_s.at[h, i], relay_r.at[h, i], place_at(0, 1 if i == 0 else 3),
                        )
                    )
                else:
                    ring[h].append(
                        send(
                            chip_out.at[part], chip_in.at[part],
                            chip_s.at[h, i], chip_r.at[h, i], chip_places[i],
                        )
                    )
            else:
                acc[h, 0:size, :] = total

    def relay(h):
        start, size = halves[h]
        for i, copy in enumerate(hops[h]):
            copy.wait_recv()
            part = (i, slice(start, start + size))
            ring[h].append(
                send(
                    relay_in.at[part], chip_in.at[part], relay_s.at[h, i], chip_r.at[h, i],
                    place_at(0, 1) if i == 0 else place_at(1, 3),
                )
            )

    def to_wire(h):
        start, size = halves[h]
        for n, copy in enumerate(ring[h]):
            copy.wait_recv()
            i = n + 2 if n < chips - 3 else n - (chips - 3)
            acc[h, 0:size, :] += chip_in[i, start : start + size, :].astype(jnp.float32)
        return [
            send(
                acc.at[h, rows_at(peer * piece, piece)], wire_in.at[h, i],
                wire_s.at[h, i], wire_r.at[h, i], wire_places[i],
            )
            for i, peer in enumerate(wire_peers)
        ]

    def from_wire(h, wires):
        own = acc[h, rows_at(w * piece, piece), :]
        for i, copy in enumerate(wires):
            copy.wait_recv()
            own = own + wire_in[h, i]
        mine = rows_at(w * piece, piece)
        gathered[h, mine, :] = (own * scale).astype(jnp.bfloat16)
        return [
            send(
                gathered.at[h, mine], gathered.at[h, mine],
                back_s.at[h, i], back_r.at[h, i], wire_places[i],
            )
            for i in range(wire_size - 1)
        ]

    forwards = []
    outs = ({}, {})

    def chip_rows(h, dx, dy):
        return rows_at(chip_at(dx, dy) * chunk + halves[h][0], halves[h][1])

    def onward(h, n, src, rows):
        spot = o_ref.at[core, rows]
        forwards.append(send(src, spot, fwd_s.at[h, n], fwd_r.at[h, n], partner))

    def pass_on(h, kind, src, rows, peer):
        outs[h][kind] = send(
            src, o_ref.at[core, rows], out_s.at[h, kind], out_r.at[h, kind], peer
        )

    def to_chips(h, back):
        for copy in back:
            copy.wait_recv()
        full = gathered.at[h, 0 : halves[h][1]]
        rows = chip_rows(h, 0, 0)
        pass_on(h, 0, full, rows, place_at(1, 0))
        pass_on(h, 1, full, rows, place_at(0, 1))
        pass_on(h, 2, full, rows, place_at(0, 3))
        onward(h, 7, full, rows)
        o_ref[core, rows, :] = gathered[h, 0 : halves[h][1], :]

    def arrived(h, kind, dx, dy):
        outs[h][kind].wait_recv()
        rows = chip_rows(h, dx, dy)
        part = o_ref.at[core, rows]
        return part, rows

    convolve(0, w2_ref, cols_m)
    relay(0)
    columns(sizes, 1, mid, halos2, padded, edge, shifted, cols_g)
    relay(1)
    wires0 = to_wire(0)
    convolve(1, w1f, cols_g)
    wires1 = to_wire(1)
    back0 = from_wire(0, wires0)
    back1 = from_wire(1, wires1)
    to_chips(0, back0)
    to_chips(1, back1)
    for h in range(2):
        part, rows = arrived(h, 0, 1, 0)
        pass_on(h, 3, part, rows, place_at(0, 1))
        pass_on(h, 4, part, rows, place_at(0, 3))
        onward(h, 0, part, rows)
        part, rows = arrived(h, 1, 0, 3)
        if h == 0:
            pass_on(h, 5, part, rows, place_at(0, 1))
        onward(h, 1, part, rows)
        part, rows = arrived(h, 2, 0, 1)
        if h == 1:
            pass_on(h, 5, part, rows, place_at(0, 3))
        onward(h, 2, part, rows)
    for h in range(2):
        part, rows = arrived(h, 5, 0, 2)
        pass_on(h, 6, part, rows, place_at(1, 0))
        onward(h, 5, part, rows)
        part, rows = arrived(h, 3, 1, 3)
        onward(h, 3, part, rows)
        part, rows = arrived(h, 4, 1, 1)
        onward(h, 4, part, rows)
    for h in range(2):
        part, rows = arrived(h, 6, 1, 2)
        onward(h, 6, part, rows)
    for copy in forwards:
        copy.wait_recv()
    sent = pair + hops[0] + hops[1] + ring[0] + ring[1] + wires0 + wires1 + back0 + back1 + forwards
    sent = sent + list(outs[0].values()) + list(outs[1].values())
    for copy in sent:
        copy.wait_send()


def halves_of(chunk):
    first = (chunk // 16 + 1) // 2 * 16
    return ((0, first), (first, chunk - first))


def work_scratch():
    return [
        pltpu.VMEM((1360, C), jnp.float32),
        pltpu.VMEM((112, C), jnp.float32),
        pltpu.VMEM((14, 96, C), jnp.bfloat16),
        pltpu.VMEM((TAPS * C, C), jnp.bfloat16),
        pltpu.VMEM((ROWS, TAPS * C), jnp.bfloat16),
    ]


def run(sizes, scale, first_weight, second_weight, dense, mask):
    drift_size, wire_size = sizes
    chips = drift_size // 2
    chunk = TAPS * C // chips
    piece = -(-halves_of(chunk)[0][1] // (wire_size * 16)) * 16
    vmem = pl.BlockSpec(memory_space=pltpu.VMEM)
    dma = pltpu.SemaphoreType.DMA
    return pl.pallas_call(
        functools.partial(kernel, sizes, scale),
        out_shape=[
            jax.ShapeDtypeStruct((2, ROWS, C), jnp.bfloat16),
            jax.ShapeDtypeStruct((2, TAPS * C, C), jnp.bfloat16),
        ],
        in_specs=[vmem] * 7,
        out_specs=[vmem] * 2,
        scratch_shapes=halo_scratch()
        + halo_scratch()
        + work_scratch()
        + [
            pltpu.VMEM((TAPS * C, C), jnp.bfloat16),
            pltpu.VMEM((ROWS, TAPS * C), jnp.bfloat16),
            pltpu.VMEM((C, ROWS), jnp.bfloat16),
            pltpu.VMEM((C, ROWS), jnp.bfloat16),
            pltpu.VMEM((2, ROWS, C), jnp.bfloat16),
            pltpu.VMEM((2, ROWS, C), jnp.float32),
            pltpu.VMEM((2, 2 * PLANES, C), jnp.bfloat16),
            pltpu.VMEM((4, 8, C), jnp.float32),
            pltpu.VMEM((4, 8, C), jnp.bfloat16),
            pltpu.VMEM((2, TAPS * C, C), jnp.float32),
            pltpu.VMEM((TAPS * C, C), jnp.float32),
            pltpu.VMEM((chips - 1, chunk, C), jnp.bfloat16),
            pltpu.VMEM((chips - 1, chunk, C), jnp.bfloat16),
            pltpu.VMEM((2, chunk, C), jnp.bfloat16),
            pltpu.VMEM((2, piece * wire_size, C), jnp.float32),
            pltpu.VMEM((2, wire_size - 1, piece, C), jnp.float32),
            pltpu.VMEM((2, piece * wire_size, C), jnp.bfloat16),
            dma((3,)), dma((3,)),
            dma((2, chips - 1)), dma((2, chips - 1)),
            dma((2, 2)), dma((2, 2)),
            dma((2, wire_size - 1)), dma((2, wire_size - 1)),
            dma((2, wire_size - 1)), dma((2, wire_size - 1)),
            dma((2, chips - 1)), dma((2, chips - 1)),
            dma((2, chips)), dma((2, chips)),
        ],
        compiler_params=pltpu.CompilerParams(
            collective_id=0, has_side_effects=True, vmem_limit_bytes=52 << 20
        ),
        name="layers",
    )(dense.reshape(2, ROWS, C), *faces(dense), first_weight, second_weight, mask)


def on_device(features, first_weight, second_weight, cotangent, counts, kernel_map, send_lists):
    sizes = (lax.axis_size("drift"), lax.axis_size("wire"))
    lists = send_lists[0, 0]
    count = counts[0, 0]
    spread = jnp.sum(jnp.where(LISTED, lists[None, :], 0), axis=1)
    active_around = (spread < 9) & AROUND
    centre = jnp.where(
        count > jnp.sum(active_around.astype(jnp.int32)),
        jnp.sum((active_around & BEFORE).astype(jnp.int32)),
        9,
    )
    slots = jnp.where(AROUND, spread, centre)
    live_pos = slots < 9

    both = jnp.stack([features[0, 0], cotangent[0, 0]]).reshape(2, 9, 64, C)
    picked = jnp.take(both, jnp.minimum(slots, 8), axis=1)
    picked = jnp.where(live_pos[None, :, None, None], picked, jnp.zeros_like(picked))
    dense = picked.reshape(2, 3, 3, 4, 4, 4, C).transpose(0, 1, 3, 5, 2, 4, 6)
    dense = jnp.pad(dense.reshape(2, 12, 4, 12, C), ((0, 0), (0, 0), (0, 0), (1, 3), (0, 0)))

    mask = jnp.broadcast_to(live_pos.reshape(3, 1, 1, 3, 1, 1), (3, 4, 4, 3, 4, C))
    mask = jnp.pad(
        mask.astype(jnp.float32).reshape(12, 4, 12, C), ((0, 0), (0, 0), (1, 3), (0, 0))
    ).reshape(ROWS, C)

    first_rows = first_weight.reshape(TAPS * C, C)
    second_rows = second_weight.reshape(TAPS * C, C)
    scale = 1.0 / math.sqrt(float(sizes[0] * sizes[1] * 576))
    summed, reduced = run(sizes, scale, first_rows, second_rows, dense, mask)

    blocks = summed.reshape(2, 3, 4, 4, 16, C)[:, :, :, :, 1:13]
    blocks = blocks.reshape(2, 3, 4, 4, 3, 4, C).transpose(0, 1, 4, 2, 5, 3, 6)
    blocks = blocks.reshape(2, 9, 64, C)
    slot_ids = jnp.arange(9, dtype=jnp.int32)
    matches = slots[None, :] == slot_ids[:, None]
    positions = jnp.sum(jnp.where(matches, slot_ids[None, :], 0), axis=1)
    placed = jnp.take(blocks, positions, axis=1)
    placed = jnp.where((slot_ids < count)[None, :, None, None], placed, jnp.zeros_like(placed))
    placed = placed.reshape(2, 1, 1, 576, C)
    weights = reduced.astype(jnp.float32).reshape(2, TAPS, C, C)
    return placed[0], placed[1], weights[0], weights[1]


def solution(mesh):
    placed = (
        P("drift", "wire", None, None),
        P(),
        P(),
        P("drift", "wire", None, None),
        P("drift", "wire"),
        P("drift", "wire", None, None),
        P("drift", "wire", None),
    )
    return jax.shard_map(
        on_device,
        mesh=mesh,
        in_specs=placed,
        out_specs=(P("drift", "wire", None, None), P("drift", "wire", None, None), P(), P()),
        check_vma=False,
    )
```

```python
import functools
import math

import jax
import jax.numpy as jnp
import numpy as np
from jax import lax
from jax.experimental import pallas as pl
from jax.experimental.pallas import tpu as pltpu
from jax.sharding import PartitionSpec as P

C = 128
PLANES = 12 * 4
ROWS = PLANES * 16
TAPS = 27
LISTED = np.arange(16)[None, :] == np.array([0, 1, 2, 7, -1, 10, 3, 4, 5])[:, None]
AROUND = np.arange(9) != 4
BEFORE = np.arange(9) < 4
MESH = pl.DeviceIdType.MESH
NEIGHBOURS = ((-1, 0), (1, 0), (0, -1), (0, 1), (-1, -1), (-1, 1), (1, -1), (1, 1))


def place(drift, wire):
    return (drift, wire)


def greet(peers):
    barrier = pltpu.get_barrier_semaphore()
    for peer in peers:
        pl.semaphore_signal(barrier, inc=1, device_id=peer, device_id_type=MESH)
    pl.semaphore_wait(barrier, len(peers))


def halo_peers(sizes):
    d = lax.axis_index("drift")
    w = lax.axis_index("wire")
    return [
        place(lax.rem(d + dd + sizes[0], sizes[0]), lax.rem(w + ww + sizes[1], sizes[1]))
        for dd, ww in NEIGHBOURS
    ]


def halo_start(peers, sends, halos, send_sem, recv_sem):
    copies = []
    for n, peer in enumerate(peers):
        which, slot = (0, n) if n < 2 else (1, n - 2) if n < 4 else (2, n - 4)
        copy = pltpu.make_async_remote_copy(
            src_ref=sends[which][slot],
            dst_ref=halos[which].at[slot],
            send_sem=send_sem.at[n],
            recv_sem=recv_sem.at[n],
            device_id=peer,
            device_id_type=MESH,
        )
        copy.start()
        copies.append(copy)
    return copies


def halo_scratch():
    return [
        pltpu.VMEM((2, 2, 64, C), jnp.bfloat16),
        pltpu.VMEM((2, 2 * PLANES, C), jnp.bfloat16),
        pltpu.VMEM((4, 8, C), jnp.bfloat16),
        pltpu.SemaphoreType.DMA((8,)),
        pltpu.SemaphoreType.DMA((8,)),
    ]


def faces(fields):
    x_send = jnp.stack([fields[:, 0], fields[:, 11]]).reshape(2, 2, 64, C)
    y_send = jnp.stack([fields[:, :, :, 1], fields[:, :, :, 12]]).reshape(2, 2 * PLANES, C)
    c_send = jnp.stack(
        [fields[:, x, :, y] for x in (0, 11) for y in (1, 12)]
    ).reshape(4, 8, C)
    return x_send, y_send, c_send


def flip(weight, out):
    for k in range(TAPS):
        tap = weight[(26 - k) * C : (27 - k) * C, :].astype(jnp.float32)
        out[k * C : (k + 1) * C, :] = tap.T.astype(jnp.bfloat16)


def columns(sizes, field, own, halos, padded, edge, shifted, out):
    x_got, y_got, c_got = halos
    d = lax.axis_index("drift")
    w = lax.axis_index("wire")
    d_ok = (d > 0, d < sizes[0] - 1)
    w_ok = (w > 0, w < sizes[1] - 1)

    def keep(value, ok):
        value = value.astype(jnp.float32)
        return jnp.where(ok, value, jnp.zeros_like(value))

    padded[...] = jnp.zeros_like(padded)
    for x in range(14):
        start = 8 + (x * 6 + 1) * 16
        if x == 0:
            value = keep(x_got[1, field], d_ok[0])
        elif x == 13:
            value = keep(x_got[0, field], d_ok[1])
        else:
            value = own[field, (x - 1) * 64 : x * 64, :].astype(jnp.float32)
        padded[start : start + 64, :] = value
    for side in range(2):
        edge[0:96, :] = keep(y_got[1 - side], w_ok[side])
        edge[96:104, :] = keep(c_got[3 - side], d_ok[0] & w_ok[side])
        edge[104:112, :] = keep(c_got[1 - side], d_ok[1] & w_ok[side])
        for x in range(14):
            first = 96 if x == 0 else 104 if x == 13 else field * PLANES + (x - 1) * 4
            first = first + (field * 4 if x in (0, 13) else 0)
            start = 8 + (x * 6 + 1) * 16 + 13 * side
            padded[pl.ds(start, 4, stride=16), :] = edge[first : first + 4, :]
    for oy in range(3):
        shifted[...] = padded[7 + oy : 7 + oy + 1344, :].astype(jnp.bfloat16).reshape(14, 96, C)
        for ox in range(3):
            for oz in range(3):
                k = 9 * ox + 3 * oy + oz
                out[:, k * C : (k + 1) * C] = shifted[
                    ox : ox + 12, oz * 16 : oz * 16 + 64, :
                ].reshape(ROWS, C)


def kernel(
    sizes, scale, own_ref, x_ref, y_ref, c_ref, w1_ref, w2_ref, mask_ref, out_ref, o_ref,
    x_got, y_got, c_got, halo_s, halo_r, x_got2, y_got2, c_got2, halo_s2, halo_r2,
    padded, edge, shifted, w1f, cols_m, w2f, cols_g, hid_t, bp_t, mid, wide, y_out, corner, c_out,
    grads, pair_in, chip_out, chip_in, acc, wire_in, gathered,
    pair_s, pair_r, chip_s, chip_r, wire_s, wire_r, back_s, back_r, out_s, out_r, fwd_s, fwd_r,
):
    drift_size, wire_size = sizes
    chips = drift_size // 2
    chunk = TAPS * C // chips
    halves = halves_of(chunk)
    piece = wire_in.shape[2]
    d = lax.axis_index("drift")
    w = lax.axis_index("wire")
    core = lax.rem(d, 2)
    chip = d // 2
    partner = place(d + 1 - 2 * core, w)
    chip_peers = [lax.rem(chip + 1 + i, chips) for i in range(chips)]
    wire_peers = [lax.rem(w + 1 + i, wire_size) for i in range(wire_size - 1)]
    chip_places = [place(2 * peer + core, w) for peer in chip_peers[:-1]]
    wire_places = [place(d, peer) for peer in wire_peers]
    near = halo_peers(sizes)
    greet([partner] + chip_places + wire_places + near)

    def send(src, dst, send_sem, recv_sem, peer):
        copy = pltpu.make_async_remote_copy(
            src_ref=src, dst_ref=dst, send_sem=send_sem, recv_sem=recv_sem,
            device_id=peer, device_id_type=MESH,
        )
        copy.start()
        return copy

    def rows_at(start, size):
        return pl.ds(pl.multiple_of(start, 16), size)

    halos = (x_got, y_got, c_got)
    first_halo = halo_start(
        near,
        ([x_ref.at[n] for n in range(2)], [y_ref.at[n] for n in range(2)],
         [c_ref.at[n] for n in range(4)]),
        halos, halo_s, halo_r,
    )
    flip(w2_ref, w2f)
    flip(w1_ref, w1f)
    acc[...] = jnp.zeros_like(acc)
    for copy in first_halo:
        copy.wait()
    columns(sizes, 0, own_ref, halos, padded, edge, shifted, cols_m)
    columns(sizes, 1, own_ref, halos, padded, edge, shifted, cols_g)

    def rows_step(i, carry):
        rows = pl.ds(pl.multiple_of(i * 256, 256), 256)
        pre = jnp.dot(cols_m[rows, :], w1_ref[...], preferred_element_type=jnp.float32)
        back = jnp.dot(cols_g[rows, :], w2f[...], preferred_element_type=jnp.float32)
        live = mask_ref[rows, :] > 0
        gate = 1.0 / (1.0 + jnp.exp(-pre))
        hid = jnp.where(live, pre / (1.0 + jnp.exp(-pre)), 0.0)
        bp = jnp.where(live, back * (gate * (1.0 + pre * (1.0 - gate))), 0.0)
        mid[0, rows, :] = hid.astype(jnp.bfloat16)
        mid[1, rows, :] = bp.astype(jnp.bfloat16)
        wide[0, rows, :] = hid
        wide[1, rows, :] = bp
        hid_t[:, rows] = hid.T.astype(jnp.bfloat16)
        bp_t[:, rows] = bp.T.astype(jnp.bfloat16)
        return carry

    lax.fori_loop(0, ROWS // 256, rows_step, 0)

    for side in range(2):
        for field in range(2):
            face = wide[field, pl.ds(1 + 11 * side, PLANES, stride=16), :]
            y_out[side, field * PLANES : (field + 1) * PLANES, :] = face.astype(jnp.bfloat16)
            corner[side, field * 4 : field * 4 + 4, :] = wide[
                field, pl.ds(1 + 11 * side, 4, stride=16), :
            ]
            corner[2 + side, field * 4 : field * 4 + 4, :] = wide[
                field, pl.ds(704 + 1 + 11 * side, 4, stride=16), :
            ]
    c_out[...] = corner[...].astype(jnp.bfloat16)
    halos2 = (x_got2, y_got2, c_got2)
    second_halo = halo_start(
        near,
        ([mid.at[:, 0:64], mid.at[:, 704:768]], [y_out.at[n] for n in range(2)],
         [c_out.at[n] for n in range(4)]),
        halos2, halo_s2, halo_r2,
    )

    def taps_step(j, carry):
        lanes = pl.ds(pl.multiple_of(j * 3 * C, C), 3 * C)
        one = jnp.dot(bp_t[...], cols_m[:, lanes], preferred_element_type=jnp.float32)
        two = jnp.dot(hid_t[...], cols_g[:, lanes], preferred_element_type=jnp.float32)
        for t in range(3):
            k = 3 * j + t
            part = slice(t * C, (t + 1) * C)
            grads[0, pl.ds(pl.multiple_of(k * C, C), C), :] = one[:, part].T
            grads[1, pl.ds(pl.multiple_of((26 - k) * C, C), C), :] = two[:, part]
        return carry

    pair = []
    for third in range(3):
        lax.fori_loop(3 * third, 3 * third + 3, taps_step, 0)
        part = rows_at(9 * C * (core * third + (1 - core) * (2 - third)), 9 * C)
        pair.append(
            send(
                grads.at[1 - core, part], pair_in.at[part],
                pair_s.at[third], pair_r.at[third], partner,
            )
        )

    for copy in second_halo:
        copy.wait()
    columns(sizes, 0, mid, halos2, padded, edge, shifted, cols_m)
    for copy in pair:
        copy.wait_recv()

    def convolve(field, weight, cols):
        def step(i, carry):
            rows = pl.ds(pl.multiple_of(i * 256, 256), 256)
            value = jnp.dot(cols[rows, :], weight[...], preferred_element_type=jnp.float32)
            out_ref[field, rows, :] = (own_ref[field, rows, :].astype(jnp.float32) + value).astype(
                jnp.bfloat16
            )
            return carry

        lax.fori_loop(0, ROWS // 256, step, 0)

    ring = ([], [])
    for h, (start, size) in enumerate(halves):
        for i, peer in enumerate(chip_peers):
            rows = rows_at(peer * chunk + start, size)
            total = grads[core, rows, :] + pair_in[rows, :]
            if i < chips - 1:
                chip_out[i, start : start + size, :] = total.astype(jnp.bfloat16)
                part = (i, slice(start, start + size))
                ring[h].append(
                    send(
                        chip_out.at[part], chip_in.at[part],
                        chip_s.at[h, i], chip_r.at[h, i], chip_places[i],
                    )
                )
            else:
                acc[h, 0:size, :] = total

    def to_wire(h):
        size = halves[h][1]
        for i, copy in enumerate(ring[h]):
            copy.wait_recv()
            start = halves[h][0]
            acc[h, 0:size, :] += chip_in[i, start : start + size, :].astype(jnp.float32)
        return [
            send(
                acc.at[h, rows_at(peer * piece, piece)], wire_in.at[h, i],
                wire_s.at[h, i], wire_r.at[h, i], wire_places[i],
            )
            for i, peer in enumerate(wire_peers)
        ]

    def from_wire(h, wires):
        own = acc[h, rows_at(w * piece, piece), :]
        for i, copy in enumerate(wires):
            copy.wait_recv()
            own = own + wire_in[h, i]
        mine = rows_at(w * piece, piece)
        gathered[h, mine, :] = (own * scale).astype(jnp.bfloat16)
        return [
            send(
                gathered.at[h, mine], gathered.at[h, mine],
                back_s.at[h, i], back_r.at[h, i], wire_places[i],
            )
            for i in range(wire_size - 1)
        ]

    def to_chips(h, back):
        for copy in back:
            copy.wait_recv()
        start, size = halves[h]
        full = gathered.at[h, 0:size]
        rows = rows_at(chip * chunk + start, size)
        spot = o_ref.at[core, rows]
        sent = [
            send(full, spot, out_s.at[h, i], out_r.at[h, i], chip_places[i])
            for i in range(chips - 1)
        ]
        ahead = send(full, spot, fwd_s.at[h, chips - 1], fwd_r.at[h, chips - 1], partner)
        o_ref[core, rows, :] = gathered[h, 0:size, :]
        return sent, [ahead]

    convolve(0, w2_ref, cols_m)
    wires0 = to_wire(0)
    columns(sizes, 1, mid, halos2, padded, edge, shifted, cols_g)
    convolve(1, w1f, cols_g)
    back0 = from_wire(0, wires0)
    wires1 = to_wire(1)
    outs0, forwards0 = to_chips(0, back0)
    back1 = from_wire(1, wires1)
    outs1, forwards1 = to_chips(1, back1)
    forwards = forwards0 + forwards1
    for h, outs in enumerate((outs0, outs1)):
        start, size = halves[h]
        for i in range(chips - 1):
            outs[i].wait_recv()
            source = lax.rem(chip + 2 * chips - 1 - i, chips)
            part = o_ref.at[core, rows_at(source * chunk + start, size)]
            forwards.append(send(part, part, fwd_s.at[h, i], fwd_r.at[h, i], partner))
    for copy in forwards:
        copy.wait_recv()
    sent = pair + ring[0] + ring[1] + wires0 + wires1 + back0 + back1 + outs0 + outs1 + forwards
    for copy in sent:
        copy.wait_send()


def halves_of(chunk):
    first = (chunk // 16 + 1) // 2 * 16
    return ((0, first), (first, chunk - first))


def work_scratch():
    return [
        pltpu.VMEM((1360, C), jnp.float32),
        pltpu.VMEM((112, C), jnp.float32),
        pltpu.VMEM((14, 96, C), jnp.bfloat16),
        pltpu.VMEM((TAPS * C, C), jnp.bfloat16),
        pltpu.VMEM((ROWS, TAPS * C), jnp.bfloat16),
    ]


def run(sizes, scale, first_weight, second_weight, dense, mask):
    drift_size, wire_size = sizes
    chips = drift_size // 2
    chunk = TAPS * C // chips
    piece = -(-halves_of(chunk)[0][1] // (wire_size * 16)) * 16
    vmem = pl.BlockSpec(memory_space=pltpu.VMEM)
    dma = pltpu.SemaphoreType.DMA
    return pl.pallas_call(
        functools.partial(kernel, sizes, scale),
        out_shape=[
            jax.ShapeDtypeStruct((2, ROWS, C), jnp.bfloat16),
            jax.ShapeDtypeStruct((2, TAPS * C, C), jnp.bfloat16),
        ],
        in_specs=[vmem] * 7,
        out_specs=[vmem] * 2,
        scratch_shapes=halo_scratch()
        + halo_scratch()
        + work_scratch()
        + [
            pltpu.VMEM((TAPS * C, C), jnp.bfloat16),
            pltpu.VMEM((ROWS, TAPS * C), jnp.bfloat16),
            pltpu.VMEM((C, ROWS), jnp.bfloat16),
            pltpu.VMEM((C, ROWS), jnp.bfloat16),
            pltpu.VMEM((2, ROWS, C), jnp.bfloat16),
            pltpu.VMEM((2, ROWS, C), jnp.float32),
            pltpu.VMEM((2, 2 * PLANES, C), jnp.bfloat16),
            pltpu.VMEM((4, 8, C), jnp.float32),
            pltpu.VMEM((4, 8, C), jnp.bfloat16),
            pltpu.VMEM((2, TAPS * C, C), jnp.float32),
            pltpu.VMEM((TAPS * C, C), jnp.float32),
            pltpu.VMEM((chips - 1, chunk, C), jnp.bfloat16),
            pltpu.VMEM((chips - 1, chunk, C), jnp.bfloat16),
            pltpu.VMEM((2, piece * wire_size, C), jnp.float32),
            pltpu.VMEM((2, wire_size - 1, piece, C), jnp.float32),
            pltpu.VMEM((2, piece * wire_size, C), jnp.bfloat16),
            dma((3,)), dma((3,)),
            dma((2, chips - 1)), dma((2, chips - 1)),
            dma((2, wire_size - 1)), dma((2, wire_size - 1)),
            dma((2, wire_size - 1)), dma((2, wire_size - 1)),
            dma((2, chips - 1)), dma((2, chips - 1)),
            dma((2, chips)), dma((2, chips)),
        ],
        compiler_params=pltpu.CompilerParams(
            collective_id=0, has_side_effects=True, vmem_limit_bytes=52 << 20
        ),
        name="layers",
    )(dense.reshape(2, ROWS, C), *faces(dense), first_weight, second_weight, mask)


def on_device(features, first_weight, second_weight, cotangent, counts, kernel_map, send_lists):
    sizes = (lax.axis_size("drift"), lax.axis_size("wire"))
    lists = send_lists[0, 0]
    count = counts[0, 0]
    spread = jnp.sum(jnp.where(LISTED, lists[None, :], 0), axis=1)
    active_around = (spread < 9) & AROUND
    centre = jnp.where(
        count > jnp.sum(active_around.astype(jnp.int32)),
        jnp.sum((active_around & BEFORE).astype(jnp.int32)),
        9,
    )
    slots = jnp.where(AROUND, spread, centre)
    live_pos = slots < 9

    both = jnp.stack([features[0, 0], cotangent[0, 0]]).reshape(2, 9, 64, C)
    picked = jnp.take(both, jnp.minimum(slots, 8), axis=1)
    picked = jnp.where(live_pos[None, :, None, None], picked, jnp.zeros_like(picked))
    dense = picked.reshape(2, 3, 3, 4, 4, 4, C).transpose(0, 1, 3, 5, 2, 4, 6)
    dense = jnp.pad(dense.reshape(2, 12, 4, 12, C), ((0, 0), (0, 0), (0, 0), (1, 3), (0, 0)))

    mask = jnp.broadcast_to(live_pos.reshape(3, 1, 1, 3, 1, 1), (3, 4, 4, 3, 4, C))
    mask = jnp.pad(
        mask.astype(jnp.float32).reshape(12, 4, 12, C), ((0, 0), (0, 0), (1, 3), (0, 0))
    ).reshape(ROWS, C)

    first_rows = first_weight.reshape(TAPS * C, C)
    second_rows = second_weight.reshape(TAPS * C, C)
    scale = 1.0 / math.sqrt(float(sizes[0] * sizes[1] * 576))
    summed, reduced = run(sizes, scale, first_rows, second_rows, dense, mask)

    blocks = summed.reshape(2, 3, 4, 4, 16, C)[:, :, :, :, 1:13]
    blocks = blocks.reshape(2, 3, 4, 4, 3, 4, C).transpose(0, 1, 4, 2, 5, 3, 6)
    blocks = blocks.reshape(2, 9, 64, C)
    slot_ids = jnp.arange(9, dtype=jnp.int32)
    matches = slots[None, :] == slot_ids[:, None]
    positions = jnp.sum(jnp.where(matches, slot_ids[None, :], 0), axis=1)
    placed = jnp.take(blocks, positions, axis=1)
    placed = jnp.where((slot_ids < count)[None, :, None, None], placed, jnp.zeros_like(placed))
    placed = placed.reshape(2, 1, 1, 576, C)
    weights = reduced.astype(jnp.float32).reshape(2, TAPS, C, C)
    return placed[0], placed[1], weights[0], weights[1]


def solution(mesh):
    placed = (
        P("drift", "wire", None, None),
        P(),
        P(),
        P("drift", "wire", None, None),
        P("drift", "wire"),
        P("drift", "wire", None, None),
        P("drift", "wire", None),
    )
    return jax.shard_map(
        on_device,
        mesh=mesh,
        in_specs=placed,
        out_specs=(P("drift", "wire", None, None), P("drift", "wire", None, None), P(), P()),
        check_vma=False,
    )
```

```python
import functools
import math

import jax
import jax.numpy as jnp
import numpy as np
from jax import lax
from jax.experimental import pallas as pl
from jax.experimental.pallas import tpu as pltpu
from jax.sharding import PartitionSpec as P

C = 128
PLANES = 12 * 4
ROWS = PLANES * 16
TAPS = 27
LISTED = np.arange(16)[None, :] == np.array([0, 1, 2, 7, -1, 10, 3, 4, 5])[:, None]
AROUND = np.arange(9) != 4
BEFORE = np.arange(9) < 4
MESH = pl.DeviceIdType.MESH
RELATIVE = ((0, 2), (1, 2), (0, 1), (0, 3), (1, 1), (1, 3), (1, 0), (0, 0))
NEIGHBOURS = ((-1, 0), (1, 0), (0, -1), (0, 1), (-1, -1), (-1, 1), (1, -1), (1, 1))


def place(drift, wire):
    return (drift, wire)


def greet(peers):
    barrier = pltpu.get_barrier_semaphore()
    for peer in peers:
        pl.semaphore_signal(barrier, inc=1, device_id=peer, device_id_type=MESH)
    pl.semaphore_wait(barrier, len(peers))


def halo_peers(sizes):
    d = lax.axis_index("drift")
    w = lax.axis_index("wire")
    return [
        place(lax.rem(d + dd + sizes[0], sizes[0]), lax.rem(w + ww + sizes[1], sizes[1]))
        for dd, ww in NEIGHBOURS
    ]


def halo_start(peers, sends, halos, send_sem, recv_sem):
    copies = []
    for n, peer in enumerate(peers):
        which, slot = (0, n) if n < 2 else (1, n - 2) if n < 4 else (2, n - 4)
        copy = pltpu.make_async_remote_copy(
            src_ref=sends[which][slot],
            dst_ref=halos[which].at[slot],
            send_sem=send_sem.at[n],
            recv_sem=recv_sem.at[n],
            device_id=peer,
            device_id_type=MESH,
        )
        copy.start()
        copies.append(copy)
    return copies


def halo_scratch():
    return [
        pltpu.VMEM((2, 2, 64, C), jnp.bfloat16),
        pltpu.VMEM((2, 2 * PLANES, C), jnp.bfloat16),
        pltpu.VMEM((4, 8, C), jnp.bfloat16),
        pltpu.SemaphoreType.DMA((8,)),
        pltpu.SemaphoreType.DMA((8,)),
    ]


def faces(fields):
    x_send = jnp.stack([fields[:, 0], fields[:, 11]]).reshape(2, 2, 64, C)
    y_send = jnp.stack([fields[:, :, :, 1], fields[:, :, :, 12]]).reshape(2, 2 * PLANES, C)
    c_send = jnp.stack(
        [fields[:, x, :, y] for x in (0, 11) for y in (1, 12)]
    ).reshape(4, 8, C)
    return x_send, y_send, c_send


def flip(weight, out):
    for k in range(TAPS):
        tap = weight[(26 - k) * C : (27 - k) * C, :].astype(jnp.float32)
        out[k * C : (k + 1) * C, :] = tap.T.astype(jnp.bfloat16)


def columns(sizes, field, own, halos, padded, edge, shifted, out):
    x_got, y_got, c_got = halos
    d = lax.axis_index("drift")
    w = lax.axis_index("wire")
    d_ok = (d > 0, d < sizes[0] - 1)
    w_ok = (w > 0, w < sizes[1] - 1)

    def keep(value, ok):
        value = value.astype(jnp.float32)
        return jnp.where(ok, value, jnp.zeros_like(value))

    padded[...] = jnp.zeros_like(padded)
    for x in range(14):
        start = 8 + (x * 6 + 1) * 16
        if x == 0:
            value = keep(x_got[1, field], d_ok[0])
        elif x == 13:
            value = keep(x_got[0, field], d_ok[1])
        else:
            value = own[field, (x - 1) * 64 : x * 64, :].astype(jnp.float32)
        padded[start : start + 64, :] = value
    for side in range(2):
        edge[0:96, :] = keep(y_got[1 - side], w_ok[side])
        edge[96:104, :] = keep(c_got[3 - side], d_ok[0] & w_ok[side])
        edge[104:112, :] = keep(c_got[1 - side], d_ok[1] & w_ok[side])
        for x in range(14):
            first = 96 if x == 0 else 104 if x == 13 else field * PLANES + (x - 1) * 4
            first = first + (field * 4 if x in (0, 13) else 0)
            start = 8 + (x * 6 + 1) * 16 + 13 * side
            padded[pl.ds(start, 4, stride=16), :] = edge[first : first + 4, :]
    for oy in range(3):
        shifted[...] = padded[7 + oy : 7 + oy + 1344, :].astype(jnp.bfloat16).reshape(14, 96, C)
        for ox in range(3):
            for oz in range(3):
                k = 9 * ox + 3 * oy + oz
                out[:, k * C : (k + 1) * C] = shifted[
                    ox : ox + 12, oz * 16 : oz * 16 + 64, :
                ].reshape(ROWS, C)


def kernel(
    sizes, scale, own_ref, x_ref, y_ref, c_ref, w1_ref, w2_ref, mask_ref, out_ref, o_ref,
    x_got, y_got, c_got, halo_s, halo_r, x_got2, y_got2, c_got2, halo_s2, halo_r2,
    padded, edge, shifted, w1f, cols_m, w2f, cols_g, hid_t, bp_t, mid, wide, y_out, corner, c_out,
    grads, pair_in, chip_out, chip_in, acc, wire_in, gathered,
    pair_s, pair_r, chip_s, chip_r, wire_s, wire_r, back_s, back_r, out_s, out_r, fwd_s, fwd_r,
):
    drift_size, wire_size = sizes
    chips = drift_size // 2
    chunk = TAPS * C // chips
    halves = halves_of(chunk)
    piece = wire_in.shape[2]
    d = lax.axis_index("drift")
    w = lax.axis_index("wire")
    core = lax.rem(d, 2)
    chip = d // 2
    partner = place(d + 1 - 2 * core, w)
    chip_x, chip_y = chip // 4, lax.rem(chip, 4)

    def chip_at(dx, dy):
        column = 1 - chip_x if dx else chip_x
        return column * 4 + lax.rem(chip_y + dy, 4)

    def place_at(dx, dy):
        return place(2 * chip_at(dx, dy) + core, w)

    chip_peers = [chip_at(dx, dy) for dx, dy in RELATIVE]
    wire_peers = [lax.rem(w + 1 + i, wire_size) for i in range(wire_size - 1)]
    chip_places = [place(2 * peer + core, w) for peer in chip_peers[:-1]]
    wire_places = [place(d, peer) for peer in wire_peers]
    near = halo_peers(sizes)
    greet([partner] + chip_places + wire_places + near)

    def send(src, dst, send_sem, recv_sem, peer):
        copy = pltpu.make_async_remote_copy(
            src_ref=src, dst_ref=dst, send_sem=send_sem, recv_sem=recv_sem,
            device_id=peer, device_id_type=MESH,
        )
        copy.start()
        return copy

    def rows_at(start, size):
        return pl.ds(pl.multiple_of(start, 16), size)

    halos = (x_got, y_got, c_got)
    first_halo = halo_start(
        near,
        ([x_ref.at[n] for n in range(2)], [y_ref.at[n] for n in range(2)],
         [c_ref.at[n] for n in range(4)]),
        halos, halo_s, halo_r,
    )
    flip(w2_ref, w2f)
    flip(w1_ref, w1f)
    acc[...] = jnp.zeros_like(acc)
    for copy in first_halo:
        copy.wait()
    columns(sizes, 0, own_ref, halos, padded, edge, shifted, cols_m)
    columns(sizes, 1, own_ref, halos, padded, edge, shifted, cols_g)

    def rows_step(i, carry):
        rows = pl.ds(pl.multiple_of(i * 256, 256), 256)
        pre = jnp.dot(cols_m[rows, :], w1_ref[...], preferred_element_type=jnp.float32)
        back = jnp.dot(cols_g[rows, :], w2f[...], preferred_element_type=jnp.float32)
        live = mask_ref[rows, :] > 0
        gate = 1.0 / (1.0 + jnp.exp(-pre))
        hid = jnp.where(live, pre / (1.0 + jnp.exp(-pre)), 0.0)
        bp = jnp.where(live, back * (gate * (1.0 + pre * (1.0 - gate))), 0.0)
        mid[0, rows, :] = hid.astype(jnp.bfloat16)
        mid[1, rows, :] = bp.astype(jnp.bfloat16)
        wide[0, rows, :] = hid
        wide[1, rows, :] = bp
        hid_t[:, rows] = hid.T.astype(jnp.bfloat16)
        bp_t[:, rows] = bp.T.astype(jnp.bfloat16)
        return carry

    lax.fori_loop(0, ROWS // 256, rows_step, 0)

    for side in range(2):
        for field in range(2):
            face = wide[field, pl.ds(1 + 11 * side, PLANES, stride=16), :]
            y_out[side, field * PLANES : (field + 1) * PLANES, :] = face.astype(jnp.bfloat16)
            corner[side, field * 4 : field * 4 + 4, :] = wide[
                field, pl.ds(1 + 11 * side, 4, stride=16), :
            ]
            corner[2 + side, field * 4 : field * 4 + 4, :] = wide[
                field, pl.ds(704 + 1 + 11 * side, 4, stride=16), :
            ]
    c_out[...] = corner[...].astype(jnp.bfloat16)
    halos2 = (x_got2, y_got2, c_got2)
    second_halo = halo_start(
        near,
        ([mid.at[:, 0:64], mid.at[:, 704:768]], [y_out.at[n] for n in range(2)],
         [c_out.at[n] for n in range(4)]),
        halos2, halo_s2, halo_r2,
    )

    def taps_step(j, carry):
        lanes = pl.ds(pl.multiple_of(j * 3 * C, C), 3 * C)
        one = jnp.dot(bp_t[...], cols_m[:, lanes], preferred_element_type=jnp.float32)
        two = jnp.dot(hid_t[...], cols_g[:, lanes], preferred_element_type=jnp.float32)
        for t in range(3):
            k = 3 * j + t
            part = slice(t * C, (t + 1) * C)
            grads[0, pl.ds(pl.multiple_of(k * C, C), C), :] = one[:, part].T
            grads[1, pl.ds(pl.multiple_of((26 - k) * C, C), C), :] = two[:, part]
        return carry

    pair = []
    for third in range(3):
        lax.fori_loop(3 * third, 3 * third + 3, taps_step, 0)
        part = rows_at(9 * C * (core * third + (1 - core) * (2 - third)), 9 * C)
        pair.append(
            send(
                grads.at[1 - core, part], pair_in.at[part],
                pair_s.at[third], pair_r.at[third], partner,
            )
        )

    for copy in second_halo:
        copy.wait()
    columns(sizes, 0, mid, halos2, padded, edge, shifted, cols_m)
    for copy in pair:
        copy.wait_recv()

    def convolve(field, weight, cols):
        def step(i, carry):
            rows = pl.ds(pl.multiple_of(i * 256, 256), 256)
            value = jnp.dot(cols[rows, :], weight[...], preferred_element_type=jnp.float32)
            out_ref[field, rows, :] = (own_ref[field, rows, :].astype(jnp.float32) + value).astype(
                jnp.bfloat16
            )
            return carry

        lax.fori_loop(0, ROWS // 256, step, 0)

    ring = ([], [])
    for h, (start, size) in enumerate(halves):
        for i, peer in enumerate(chip_peers):
            rows = rows_at(peer * chunk + start, size)
            total = grads[core, rows, :] + pair_in[rows, :]
            if i < chips - 1:
                chip_out[i, start : start + size, :] = total.astype(jnp.bfloat16)
                part = (i, slice(start, start + size))
                ring[h].append(
                    send(
                        chip_out.at[part], chip_in.at[part],
                        chip_s.at[h, i], chip_r.at[h, i], chip_places[i],
                    )
                )
            else:
                acc[h, 0:size, :] = total

    def to_wire(h):
        size = halves[h][1]
        for i, copy in enumerate(ring[h]):
            copy.wait_recv()
            start = halves[h][0]
            acc[h, 0:size, :] += chip_in[i, start : start + size, :].astype(jnp.float32)
        return [
            send(
                acc.at[h, rows_at(peer * piece, piece)], wire_in.at[h, i],
                wire_s.at[h, i], wire_r.at[h, i], wire_places[i],
            )
            for i, peer in enumerate(wire_peers)
        ]

    def from_wire(h, wires):
        own = acc[h, rows_at(w * piece, piece), :]
        for i, copy in enumerate(wires):
            copy.wait_recv()
            own = own + wire_in[h, i]
        mine = rows_at(w * piece, piece)
        gathered[h, mine, :] = (own * scale).astype(jnp.bfloat16)
        return [
            send(
                gathered.at[h, mine], gathered.at[h, mine],
                back_s.at[h, i], back_r.at[h, i], wire_places[i],
            )
            for i in range(wire_size - 1)
        ]

    forwards = []
    outs = ({}, {})

    def chip_rows(h, dx, dy):
        return rows_at(chip_at(dx, dy) * chunk + halves[h][0], halves[h][1])

    def onward(h, n, src, rows):
        spot = o_ref.at[core, rows]
        forwards.append(send(src, spot, fwd_s.at[h, n], fwd_r.at[h, n], partner))

    def pass_on(h, kind, src, rows, peer):
        outs[h][kind] = send(
            src, o_ref.at[core, rows], out_s.at[h, kind], out_r.at[h, kind], peer
        )

    def to_chips(h, back):
        for copy in back:
            copy.wait_recv()
        full = gathered.at[h, 0 : halves[h][1]]
        rows = chip_rows(h, 0, 0)
        pass_on(h, 0, full, rows, place_at(1, 0))
        pass_on(h, 1, full, rows, place_at(0, 1))
        pass_on(h, 2, full, rows, place_at(0, 3))
        onward(h, 7, full, rows)
        o_ref[core, rows, :] = gathered[h, 0 : halves[h][1], :]

    def arrived(h, kind, dx, dy):
        outs[h][kind].wait_recv()
        rows = chip_rows(h, dx, dy)
        part = o_ref.at[core, rows]
        return part, rows

    convolve(0, w2_ref, cols_m)
    wires0 = to_wire(0)
    columns(sizes, 1, mid, halos2, padded, edge, shifted, cols_g)
    convolve(1, w1f, cols_g)
    wires1 = to_wire(1)
    back0 = from_wire(0, wires0)
    back1 = from_wire(1, wires1)
    to_chips(0, back0)
    to_chips(1, back1)
    for h in range(2):
        part, rows = arrived(h, 0, 1, 0)
        pass_on(h, 3, part, rows, place_at(0, 1))
        pass_on(h, 4, part, rows, place_at(0, 3))
        onward(h, 0, part, rows)
        part, rows = arrived(h, 1, 0, 3)
        if h == 0:
            pass_on(h, 5, part, rows, place_at(0, 1))
        onward(h, 1, part, rows)
        part, rows = arrived(h, 2, 0, 1)
        if h == 1:
            pass_on(h, 5, part, rows, place_at(0, 3))
        onward(h, 2, part, rows)
    for h in range(2):
        part, rows = arrived(h, 5, 0, 2)
        pass_on(h, 6, part, rows, place_at(1, 0))
        onward(h, 5, part, rows)
        part, rows = arrived(h, 3, 1, 3)
        onward(h, 3, part, rows)
        part, rows = arrived(h, 4, 1, 1)
        onward(h, 4, part, rows)
    for h in range(2):
        part, rows = arrived(h, 6, 1, 2)
        onward(h, 6, part, rows)
    for copy in forwards:
        copy.wait_recv()
    sent = pair + ring[0] + ring[1] + wires0 + wires1 + back0 + back1 + forwards
    sent = sent + list(outs[0].values()) + list(outs[1].values())
    for copy in sent:
        copy.wait_send()


def halves_of(chunk):
    first = (chunk // 16 + 1) // 2 * 16
    return ((0, first), (first, chunk - first))


def work_scratch():
    return [
        pltpu.VMEM((1360, C), jnp.float32),
        pltpu.VMEM((112, C), jnp.float32),
        pltpu.VMEM((14, 96, C), jnp.bfloat16),
        pltpu.VMEM((TAPS * C, C), jnp.bfloat16),
        pltpu.VMEM((ROWS, TAPS * C), jnp.bfloat16),
    ]


def run(sizes, scale, first_weight, second_weight, dense, mask):
    drift_size, wire_size = sizes
    chips = drift_size // 2
    chunk = TAPS * C // chips
    piece = -(-halves_of(chunk)[0][1] // (wire_size * 16)) * 16
    vmem = pl.BlockSpec(memory_space=pltpu.VMEM)
    dma = pltpu.SemaphoreType.DMA
    return pl.pallas_call(
        functools.partial(kernel, sizes, scale),
        out_shape=[
            jax.ShapeDtypeStruct((2, ROWS, C), jnp.bfloat16),
            jax.ShapeDtypeStruct((2, TAPS * C, C), jnp.bfloat16),
        ],
        in_specs=[vmem] * 7,
        out_specs=[vmem] * 2,
        scratch_shapes=halo_scratch()
        + halo_scratch()
        + work_scratch()
        + [
            pltpu.VMEM((TAPS * C, C), jnp.bfloat16),
            pltpu.VMEM((ROWS, TAPS * C), jnp.bfloat16),
            pltpu.VMEM((C, ROWS), jnp.bfloat16),
            pltpu.VMEM((C, ROWS), jnp.bfloat16),
            pltpu.VMEM((2, ROWS, C), jnp.bfloat16),
            pltpu.VMEM((2, ROWS, C), jnp.float32),
            pltpu.VMEM((2, 2 * PLANES, C), jnp.bfloat16),
            pltpu.VMEM((4, 8, C), jnp.float32),
            pltpu.VMEM((4, 8, C), jnp.bfloat16),
            pltpu.VMEM((2, TAPS * C, C), jnp.float32),
            pltpu.VMEM((TAPS * C, C), jnp.float32),
            pltpu.VMEM((chips - 1, chunk, C), jnp.bfloat16),
            pltpu.VMEM((chips - 1, chunk, C), jnp.bfloat16),
            pltpu.VMEM((2, piece * wire_size, C), jnp.float32),
            pltpu.VMEM((2, wire_size - 1, piece, C), jnp.float32),
            pltpu.VMEM((2, piece * wire_size, C), jnp.bfloat16),
            dma((3,)), dma((3,)),
            dma((2, chips - 1)), dma((2, chips - 1)),
            dma((2, wire_size - 1)), dma((2, wire_size - 1)),
            dma((2, wire_size - 1)), dma((2, wire_size - 1)),
            dma((2, chips - 1)), dma((2, chips - 1)),
            dma((2, chips)), dma((2, chips)),
        ],
        compiler_params=pltpu.CompilerParams(
            collective_id=0, has_side_effects=True, vmem_limit_bytes=52 << 20
        ),
        name="layers",
    )(dense.reshape(2, ROWS, C), *faces(dense), first_weight, second_weight, mask)


def on_device(features, first_weight, second_weight, cotangent, counts, kernel_map, send_lists):
    sizes = (lax.axis_size("drift"), lax.axis_size("wire"))
    lists = send_lists[0, 0]
    count = counts[0, 0]
    spread = jnp.sum(jnp.where(LISTED, lists[None, :], 0), axis=1)
    active_around = (spread < 9) & AROUND
    centre = jnp.where(
        count > jnp.sum(active_around.astype(jnp.int32)),
        jnp.sum((active_around & BEFORE).astype(jnp.int32)),
        9,
    )
    slots = jnp.where(AROUND, spread, centre)
    live_pos = slots < 9

    both = jnp.stack([features[0, 0], cotangent[0, 0]]).reshape(2, 9, 64, C)
    picked = jnp.take(both, jnp.minimum(slots, 8), axis=1)
    picked = jnp.where(live_pos[None, :, None, None], picked, jnp.zeros_like(picked))
    dense = picked.reshape(2, 3, 3, 4, 4, 4, C).transpose(0, 1, 3, 5, 2, 4, 6)
    dense = jnp.pad(dense.reshape(2, 12, 4, 12, C), ((0, 0), (0, 0), (0, 0), (1, 3), (0, 0)))

    mask = jnp.broadcast_to(live_pos.reshape(3, 1, 1, 3, 1, 1), (3, 4, 4, 3, 4, C))
    mask = jnp.pad(
        mask.astype(jnp.float32).reshape(12, 4, 12, C), ((0, 0), (0, 0), (1, 3), (0, 0))
    ).reshape(ROWS, C)

    first_rows = first_weight.reshape(TAPS * C, C)
    second_rows = second_weight.reshape(TAPS * C, C)
    scale = 1.0 / math.sqrt(float(sizes[0] * sizes[1] * 576))
    summed, reduced = run(sizes, scale, first_rows, second_rows, dense, mask)

    blocks = summed.reshape(2, 3, 4, 4, 16, C)[:, :, :, :, 1:13]
    blocks = blocks.reshape(2, 3, 4, 4, 3, 4, C).transpose(0, 1, 4, 2, 5, 3, 6)
    blocks = blocks.reshape(2, 9, 64, C)
    slot_ids = jnp.arange(9, dtype=jnp.int32)
    matches = slots[None, :] == slot_ids[:, None]
    positions = jnp.sum(jnp.where(matches, slot_ids[None, :], 0), axis=1)
    placed = jnp.take(blocks, positions, axis=1)
    placed = jnp.where((slot_ids < count)[None, :, None, None], placed, jnp.zeros_like(placed))
    placed = placed.reshape(2, 1, 1, 576, C)
    weights = reduced.astype(jnp.float32).reshape(2, TAPS, C, C)
    return placed[0], placed[1], weights[0], weights[1]


def solution(mesh):
    placed = (
        P("drift", "wire", None, None),
        P(),
        P(),
        P("drift", "wire", None, None),
        P("drift", "wire"),
        P("drift", "wire", None, None),
        P("drift", "wire", None),
    )
    return jax.shard_map(
        on_device,
        mesh=mesh,
        in_specs=placed,
        out_specs=(P("drift", "wire", None, None), P("drift", "wire", None, None), P(), P()),
        check_vma=False,
    )
```
